32 devices in a mesh: section: 4 (over y, x), tile: 8 (over z, core).
Axes of the slice: x: 2, y: 2, z: 4, core: 2. Of those that a mesh axis runs over, the one named last changes fastest.
Arguments:
- latents: bfloat16 [16, 8, 4, 24, 384], P('section', 'tile'), may hold values from -6 to 6
- frame_counts: int32 [4], replicated, may hold values from 2 to 4, as said below
- norm_gain: float32 [384], replicated, may hold values from 0.1 to 1.9
- conv_weight: bfloat16 [3, 3, 3, 384, 384], replicated, may hold values from -0.0625 to 0.0625
- up_weight: bfloat16 [3, 3, 384, 192], replicated, may hold values from -0.109375 to 0.109375
- pixel_grad: bfloat16 [16, 8, 8, 24, 384], P('section', 'tile'), may hold values from -6 to 6
Outputs:
- decoded: bfloat16 [16, 8, 8, 24, 384], P('section', 'tile')
- latent_grad: float32 [16, 8, 4, 24, 384], P('section', 'tile')
The draws below stay inside these ranges and needn't reach their ends.
Inputs may be any that keep to these rules, and one draw needn't show every extreme that they name: `frame_counts`: every group has at least two frames; some group is full in every draw.
All inputs are finite; a program needn't handle non-finite values.
Results may differ from the reference program's by a relative error of at most 0.0058.
Values may be sent and summed in bfloat16 or wider, within the bound.
A program may use at most 64 MiB of HBM per device.

```python
import jax
import jax.numpy as jnp
from jax import lax

C = 384
C2 = 192
FMAX = 4
GCOL = 4
BR = 4
BW = 24
GROUPS = 4
FRAMES = 16
N_TILE = 8


def draw_frame_counts(key, part):
    first, second = jax.random.split(key)
    counts = jax.random.randint(first, (GROUPS,), 2, FMAX + 1)
    fullest = jax.random.randint(second, (), 0, GROUPS)
    return jnp.where(jnp.arange(GROUPS) == fullest, FMAX, counts).astype(jnp.int32)


def block_levels(rng, extent, cuts, low, top_value):
    def one(axis_at, shards_of):
        heights = jax.random.uniform(jax.random.fold_in(jax.random.fold_in(rng, 6), axis_at), (shards_of,), jnp.float32, low / len(cuts), top_value / len(cuts))
        return jnp.repeat(jnp.exp(heights), extent[axis_at] // shards_of).reshape((-1,) + (1,) * (len(extent) - axis_at - 1))

    factor_of = one(*cuts[0])
    for cut in cuts[1:]:
        factor_of = factor_of * one(*cut)
    return factor_of


def centred(rng, shape, scale, limit, pieces=(), held_as=jnp.bfloat16):
    result = jax.random.normal(rng, shape, jnp.float32) * scale
    if len(pieces) > 0:
        result = block_levels(rng, shape, pieces, -0.22, 0.18) * result
    return jnp.clip(result, min=-limit, max=limit).astype(held_as)


def setup_inputs(seed: int = 0) -> dict:
    seeds = jax.random.split(jax.random.key(seed), 7)
    return {
        "latents": centred(seeds[0], (FRAMES, N_TILE, BR, BW, C), 1.0, 6.0, ((0, 4), (1, 8))),
        "frame_counts": draw_frame_counts(jax.random.fold_in(seeds[6], 71), 0),
        "norm_gain": jnp.clip(1.0 + 0.18 * jax.random.normal(seeds[2], (C,), jnp.float32), 0.1, 1.9),
        "conv_weight": centred(seeds[3], (3, 3, 3, C, C), (27 * C) ** -0.5, 0.0625),
        "up_weight": centred(seeds[4], (3, 3, C, C2), (9 * C) ** -0.5, 0.109375),
        "pixel_grad": centred(seeds[5], (FRAMES, N_TILE, 2 * BR, BW, 2 * C2), 1.0, 6.0, ((0, 4), (1, 8))),
    }


EPS = 1e-06

def activate(values, gain):
    floats = values.astype(jnp.float32)
    scale = lax.rsqrt(lax.optimization_barrier(jnp.mean(floats * floats, axis=-1, keepdims=True)) + EPS)
    normed = floats * scale * gain
    return normed * jax.nn.sigmoid(normed)

def to_image(blocks):
    placed = jnp.roll(blocks, GCOL + 1, axis=1)
    frames, count, rows, cols, chans = placed.shape
    rowblocks = count // GCOL
    grid = placed.reshape(frames, rowblocks, GCOL, rows, cols, chans)
    return jnp.transpose(grid, (0, 1, 3, 2, 4, 5)).reshape(frames, rowblocks * rows, GCOL * cols, chans)

def from_image(image, rows, cols):
    frames, height, width, chans = image.shape
    rowblocks = height // rows
    grid = image.reshape(frames, rowblocks, rows, GCOL, cols, chans)
    placed = jnp.transpose(grid, (0, 1, 3, 2, 4, 5)).reshape(frames, rowblocks * GCOL, rows, cols, chans)
    return jnp.roll(placed, -(GCOL + 1), axis=1)

def conv_three(extended, weight):
    return lax.conv_general_dilated(extended[None], weight, (1, 1, 1), ((0, 0), (1, 1), (1, 1)), dimension_numbers=('NDHWC', 'DHWIO', 'NDHWC'), preferred_element_type=jnp.float32)[0]

def conv_plane(image, weight):
    return lax.conv_general_dilated(image, weight, (1, 1), ((1, 1), (1, 1)), dimension_numbers=('NHWC', 'HWIO', 'NHWC'), preferred_element_type=jnp.float32)

def place(grad_hidden, future, length):
    frames = grad_hidden.shape[0]
    padded = jnp.concatenate([grad_hidden, jnp.zeros((2,) + grad_hidden.shape[1:], grad_hidden.dtype)], 0)
    slots = jnp.arange(frames + 2, dtype=jnp.int32)[:, None, None, None]
    return jnp.where(slots == length, future[0][None], jnp.where(slots == length + 1, future[1][None], padded))

def reference(latents, frame_counts, norm_gain, conv_weight, up_weight, pixel_grad):
    groups = frame_counts.shape[0]
    frames = latents.shape[0] // groups
    rows, cols = (latents.shape[2], latents.shape[3])
    image = to_image(latents)
    grad_image = to_image(pixel_grad)
    height, width, chans = (image.shape[1], image.shape[2], image.shape[3])
    acts = activate(image, norm_gain).astype(jnp.bfloat16)
    flipped_one = jnp.transpose(jnp.flip(conv_weight, (0, 1, 2)), (0, 1, 2, 4, 3))
    flipped_two = jnp.transpose(jnp.flip(up_weight, (0, 1)), (0, 1, 3, 2))
    position = jnp.arange(frames, dtype=jnp.int32)
    cache = jnp.zeros((2, height, width, chans), jnp.bfloat16)
    decoded_parts = []
    hidden_grads = []
    masks = []
    for group in range(groups):
        length = frame_counts[group]
        mask = (position < length)[:, None, None, None]
        masks.append(mask)
        own = acts[group * frames:(group + 1) * frames]
        extended = jnp.concatenate([cache, own], 0)
        hidden = conv_three(extended, conv_weight).astype(jnp.bfloat16)
        upsampled = jnp.repeat(jnp.repeat(hidden, 2, axis=1), 2, axis=2)
        output = conv_plane(upsampled, up_weight).reshape(frames, 2 * height, width, -1)
        decoded_parts.append(jnp.where(mask, output, 0.0).astype(jnp.bfloat16))
        cache = lax.dynamic_slice_in_dim(own, (length - 2).astype(jnp.int32), 2, 0)
        grad_group = grad_image[group * frames:(group + 1) * frames]
        grad_out = jnp.where(mask, grad_group, jnp.zeros_like(grad_group))
        grad_plane = grad_out.reshape(frames, 2 * height, 2 * width, -1)
        grad_up = conv_plane(grad_plane, flipped_two)
        grad_hidden = grad_up.reshape(frames, height, 2, width, 2, chans).sum(axis=(2, 4)).astype(jnp.bfloat16)
        hidden_grads.append(grad_hidden)
    act_grads = []
    for group in range(groups):
        if group + 1 < groups:
            future = hidden_grads[group + 1][:2]
        else:
            future = jnp.zeros((2, height, width, chans), jnp.bfloat16)
        grad_ext = place(hidden_grads[group], future, frame_counts[group])
        act_grads.append(conv_three(grad_ext, flipped_one))
    grad_acts = jnp.concatenate(act_grads, 0)
    _, pull = jax.vjp(lambda values: activate(values, norm_gain), image.astype(jnp.float32))
    latent_grad = pull(grad_acts)[0]
    frame_mask = jnp.concatenate(masks, 0)
    latent_grad = jnp.where(frame_mask, latent_grad, 0.0).astype(jnp.float32)
    decoded = jnp.concatenate(decoded_parts, 0)
    return (from_image(decoded, 2 * rows, cols), from_image(latent_grad, rows, cols))
```

```python
import functools

import jax
import jax.numpy as jnp
from jax import lax
from jax.experimental import pallas as pl
from jax.experimental.pallas import tpu as pltpu
from jax.sharding import PartitionSpec as P

GCOL = 4
SHIFT = GCOL + 1
EPS = 1e-06
BF = jnp.bfloat16
F32 = jnp.float32
AROUND = [(dy, dx) for dy in (-1, 0, 1) for dx in (-1, 0, 1)]
TAPS = {-1: (2,), 0: (1, 2), 1: (0, 1), 2: (0,)}
OFFS = {0: 0, 1: 1, 2: 2, -1: 3}


def kernel(sections, tiles, counts, gain_ref, lat_h, cw_h, up_h, pg_h, dec, lg,
           lat, cwf, cwb, up, pg, comb,
           act, sel, gh, hid, ylow, ygrad, zmat, acc,
           act_top, act_bot, act_l, act_r, act_sl, act_sr,
           gh_top, gh_bot, gh_l, gh_r, gh_sl, gh_sr,
           hid_top, hid_bot, hid_l, hid_r, hid_sl, hid_sr,
           pg_top, pg_bot, pg_l, pg_r, pg_sl, pg_sr,
           load_sem, back_sem, out_sem, send_sem, recv_sem):
    frames, rows, width, chans = lat.shape
    half = up.shape[1]
    prow = 2 * rows
    cells = rows * width
    every = frames * cells
    rowblocks = tiles // GCOL
    sec = lax.axis_index("section")
    tile = lax.axis_index("tile")
    place = lax.rem(tile + SHIFT, tiles)
    brow = place // GCOL
    bcol = lax.rem(place, GCOL)

    def there(ds, dy, dx):
        return (
            (sec + ds >= 0) & (sec + ds < sections)
            & (brow + dy >= 0) & (brow + dy < rowblocks)
            & (bcol + dx >= 0) & (bcol + dx < GCOL)
        )

    def who(ds, dy, dx):
        at = lax.rem(place + GCOL * dy + dx + 2 * tiles - SHIFT, tiles)
        return {"section": sec + ds, "tile": at}

    loads = [
        pltpu.make_async_copy(pg_h, pg, load_sem.at[0]),
        pltpu.make_async_copy(lat_h, lat, load_sem.at[1]),
        pltpu.make_async_copy(up_h, up, load_sem.at[2]),
    ] + [pltpu.make_async_copy(cw_h.at[pl.ds(9 * dt, 9)], cwf.at[dt], load_sem.at[3 + dt]) for dt in range(3)]
    for load in loads:
        load.start()
    backs = []
    for dt in range(3):
        for k in range(9):
            backs.append(pltpu.make_async_copy(
                cw_h.at[9 * dt + k], cwb.at[dt, :, pl.ds((8 - k) * chans, chans)], back_sem.at[9 * dt + k]))
    for back in backs:
        back.start()

    barrier = pltpu.get_barrier_semaphore()
    near = [(ds, dy, dx) for ds in (-1, 0, 1) for dy, dx in AROUND if (ds, dy, dx) != (0, 0, 0)]
    for spot in near:
        @pl.when(there(*spot))
        def _(spot=spot):
            pl.semaphore_signal(barrier, inc=1, device_id=who(*spot), device_id_type=pl.DeviceIdType.MESH)
    pl.semaphore_wait(barrier, sum(there(*spot).astype(jnp.int32) for spot in near))

    number = [0]
    pending = []

    def message(src, dst, ds, dy, dx):
        n = number[0]
        number[0] += 1
        copy = pltpu.make_async_remote_copy(
            src_ref=src, dst_ref=dst, send_sem=send_sem.at[n], recv_sem=recv_sem.at[n],
            device_id=who(ds, dy, dx), device_id_type=pl.DeviceIdType.MESH)
        pending.append((copy, there(ds, dy, dx)))

        @pl.when(there(ds, dy, dx))
        def _():
            copy.start()

        def arrive():
            came = there(-ds, -dy, -dx)

            @pl.when(came)
            def _():
                copy.wait_recv()

            @pl.when(jnp.logical_not(came))
            def _():
                dst[...] = jnp.zeros(dst.shape, dst.dtype)

        return arrive

    def exchange(center, sl, sr, fs, halo, fd, ds, height):
        top, bot, left, right = halo
        src = pl.ds(*fs)
        csrc = center[1]
        dst = pl.ds(*fd)
        out = []
        for dy, dx in AROUND:
            if dx == 0:
                if dy == 1:
                    out.append(message(center[0].at[csrc, height - 1], top.at[dst], ds, 1, 0))
                elif dy == -1:
                    out.append(message(center[0].at[csrc, 0], bot.at[dst], ds, -1, 0))
                continue
            stage, onto = (sr, left) if dx == 1 else (sl, right)
            if dy == 0:
                out.append(message(stage.at[src], onto.at[dst, pl.ds(1, height)], ds, 0, dx))
            elif dy == 1:
                out.append(message(stage.at[src, height - 1], onto.at[dst, 0], ds, 1, dx))
            else:
                out.append(message(stage.at[src, 0], onto.at[dst, height + 1], ds, -1, dx))
        return out

    def edges(value, f, r, sl, sr):
        sl[f, r] = value[0:1]
        sr[f, r] = value[width - 1:width]

    loads[0].wait()

    def stage_pixels(f, _):
        for r in range(prow):
            edges(pg[f, r].astype(F32), f, r, pg_sl, pg_sr)
        return 0

    lax.fori_loop(0, frames, stage_pixels, 0)
    pg_in = exchange((pg, pl.ds(0, frames)), pg_sl, pg_sr, (0, frames),
                     (pg_top, pg_bot, pg_l, pg_r), (0, frames), 0, prow)

    length = sum(jnp.where(sec == i, counts[i], 0) for i in range(sections))
    gain = gain_ref[...].reshape(1, chans)
    loads[1].wait()

    def activate(f, _):
        for r in range(rows):
            x = lat[f, r].astype(F32)
            scale = lax.rsqrt(jnp.mean(x * x, axis=-1, keepdims=True) + EPS)
            v = x * scale * gain
            a = (v * jax.nn.sigmoid(v)).astype(BF)
            act[f + 2, r] = a
            edges(a.astype(F32), f + 2, r, act_sl, act_sr)
        return 0

    lax.fori_loop(0, frames, activate, 0)
    for k in range(2):
        for r in range(rows):
            total = None
            for j in range(frames):
                w = jnp.where(length - 2 + k == j, 1.0, 0.0).astype(F32)
                term = act[j + 2, r].astype(F32) * w
                total = term if total is None else total + term
            sel[k, r] = total.astype(BF)
            edges(total, k, r, act_sl, act_sr)
    act_halo = (act_top, act_bot, act_l, act_r)
    act_in = exchange((act, pl.ds(2, frames)), act_sl, act_sr, (2, frames), act_halo, (2, frames), 0, rows)
    act_in += exchange((sel, pl.ds(0, 2)), act_sl, act_sr, (0, 2), act_halo, (0, 2), 1, rows)
    act_in.append(message(sel, act.at[pl.ds(0, 2)], 1, 0, 0))

    loads[2].wait()
    for u in (-1, 0, 1, 2):
        for v in (-1, 0, 1, 2):
            total = None
            for i in TAPS[u]:
                for j in TAPS[v]:
                    term = up[3 * i + j].astype(F32)
                    total = term if total is None else total + term
            comb[pl.ds(((u + 1) * 4 + OFFS[v]) * half, half), :] = total.astype(BF)

    row_id = lax.broadcasted_iota(jnp.int32, (width, chans), 0)
    lane_id = lax.broadcasted_iota(jnp.int32, (width, chans), 1)

    def shifted(x, left, right):
        xl = jnp.where(row_id == 0, left, pltpu.roll(x, 1, axis=0))
        xr = jnp.where(row_id == width - 1, right, pltpu.roll(x, width - 1, axis=0))
        return xl, xr

    for arrive in pg_in:
        arrive()

    def pixels(f, _):
        mid, side = [], []
        for e in range(prow + 2):
            x = (pg_top[f] if e == 0 else pg_bot[f] if e == prow + 1 else pg[f, e - 1]).astype(F32)
            xl, xr = shifted(x, pg_l[f, e], pg_r[f, e])
            mid.append(x)
            side.append(jnp.where(lane_id < half, xr, xl))
        at = pl.ds(pl.multiple_of(f * cells, cells), cells)
        for u in (-1, 0, 1, 2):
            pick = [2 * r + u + 1 for r in range(rows)]
            base = (u + 1) * 2 * chans
            zmat[at, pl.ds(base, chans)] = jnp.concatenate([mid[e] for e in pick], 0).astype(BF)
            zmat[at, pl.ds(base + chans, chans)] = jnp.concatenate([side[e] for e in pick], 0).astype(BF)
        return 0

    lax.fori_loop(0, frames, pixels, 0)
    acc[...] = jnp.dot(zmat[...], comb[...], preferred_element_type=F32)

    def keep(onto, sl, sr):
        def body(f, _):
            for r in range(rows):
                x = acc[pl.ds(pl.multiple_of(f * cells + r * width, 8), width), :].astype(BF)
                onto[f, r] = x
                edges(x.astype(F32), f, r, sl, sr)
            return 0

        lax.fori_loop(0, frames, body, 0)

    keep(gh, gh_sl, gh_sr)
    gh_halo = (gh_top, gh_bot, gh_l, gh_r)
    gh_in = exchange((gh, pl.ds(0, frames)), gh_sl, gh_sr, (0, frames), gh_halo, (0, frames), 0, rows)
    gh_in += exchange((gh, pl.ds(0, 2)), gh_sl, gh_sr, (0, 2), gh_halo, (frames, 2), -1, rows)
    gh_in.append(message(gh.at[pl.ds(0, 2)], gh.at[pl.ds(frames, 2)], -1, 0, 0))

    def unfold(onto, count, center, halo, mix):
        top, bot, left, right = halo

        def body(f, _):
            xs, ls, rs = [], [], []
            for e in range(rows + 2):
                x = mix(f, lambda g: (top[g] if e == 0 else bot[g] if e == rows + 1 else center[g, e - 1]).astype(F32))
                xl, xr = shifted(x, mix(f, lambda g: left[g, e]), mix(f, lambda g: right[g, e]))
                xs.append(x)
                ls.append(xl)
                rs.append(xr)
            at = pl.ds(pl.multiple_of(f * cells, cells), cells)
            for dr in range(3):
                for dc, group in enumerate((ls, xs, rs)):
                    onto[at, pl.ds((3 * dr + dc) * chans, chans)] = jnp.concatenate(group[dr:dr + rows], 0).astype(BF)
            return 0

        lax.fori_loop(0, count, body, 0)

    def plain(f, get):
        return get(f)

    for arrive in act_in:
        arrive()
    unfold(ylow, frames + 2, act, act_halo, plain)
    for dt in range(3):
        loads[3 + dt].wait()
    total = None
    for dt in range(3):
        term = jnp.dot(ylow[pl.ds(dt * cells, every), :], cwf[dt].reshape(9 * chans, chans),
                       preferred_element_type=F32)
        total = term if total is None else total + term
    acc[...] = total
    keep(hid, hid_sl, hid_sr)
    hid_halo = (hid_top, hid_bot, hid_l, hid_r)
    hid_in = exchange((hid, pl.ds(0, frames)), hid_sl, hid_sr, (0, frames), hid_halo, (0, frames), 0, rows)

    for arrive in gh_in:
        arrive()

    def placed(f, get):
        own = jnp.where(f < length, 1.0, 0.0).astype(F32)
        one = jnp.where(f == length, 1.0, 0.0).astype(F32)
        two = jnp.where(f == length + 1, 1.0, 0.0).astype(F32)
        return get(jnp.minimum(f, frames - 1)) * own + get(frames) * one + get(frames + 1) * two

    unfold(ygrad, frames + 2, gh, gh_halo, placed)
    for back in backs:
        back.wait()
    total = None
    for dt in range(3):
        term = lax.dot_general(ygrad[pl.ds((2 - dt) * cells, every), :], cwb[dt],
                               (((1,), (1,)), ((), ())), preferred_element_type=F32)
        total = term if total is None else total + term
    acc[...] = total

    def finish(f, _):
        real = jnp.where(f < length, 1.0, 0.0).astype(F32)
        for r in range(rows):
            g = acc[pl.ds(pl.multiple_of(f * cells + r * width, 8), width), :]
            x = lat[f, r].astype(F32)
            scale = lax.rsqrt(jnp.mean(x * x, axis=-1, keepdims=True) + EPS)
            v = x * scale * gain
            s = jax.nn.sigmoid(v)
            dn = g * (s + v * s * (1.0 - s)) * gain
            dot = jnp.mean(dn * x, axis=-1, keepdims=True)
            lg[f, r] = (dn * scale - x * (scale * scale * scale * dot)) * real
        return 0

    lax.fori_loop(0, frames, finish, 0)

    for arrive in hid_in:
        arrive()
    unfold(ylow, frames, hid, hid_halo, plain)
    for a in range(2):
        parts = []
        for b in range(2):
            total = None
            for dr in (a, a + 1):
                for dc in (b, b + 1):
                    u, v = a - 2 * (dr - 1), b - 2 * (dc - 1)
                    term = lax.dot_general(
                        ylow[pl.ds(0, every), pl.ds((3 * dr + dc) * chans, chans)],
                        comb[pl.ds(((u + 1) * 4 + OFFS[v]) * half, half), :],
                        (((1,), (1,)), ((), ())), preferred_element_type=F32)
                    total = term if total is None else total + term
            parts.append(total)
        acc[...] = jnp.concatenate(parts, axis=1)

        def spread(f, _):
            real = jnp.where(f < length, 1.0, 0.0).astype(F32)
            for r in range(rows):
                x = acc[pl.ds(pl.multiple_of(f * cells + r * width, 8), width), :]
                dec[f, 2 * r + a] = (x * real).astype(BF)
            return 0

        lax.fori_loop(0, frames, spread, 0)
    for copy, went in pending:
        @pl.when(went)
        def _(copy=copy):
            copy.wait_send()


def per_device(sections, tiles, latents, frame_counts, norm_gain, conv_weight, up_weight, pixel_grad):
    frames, _, rows, width, chans = latents.shape
    half = up_weight.shape[-1]
    prow = 2 * rows
    cells = rows * width
    every = frames * cells
    tall = frames + 2

    def rims(count, height):
        return [
            pltpu.VMEM((count, width, chans), BF),
            pltpu.VMEM((count, width, chans), BF),
            pltpu.VMEM((count, height + 2, 1, chans), F32),
            pltpu.VMEM((count, height + 2, 1, chans), F32),
            pltpu.VMEM((count, height, 1, chans), F32),
            pltpu.VMEM((count, height, 1, chans), F32),
        ]

    decoded, latent_grad = pl.pallas_call(
        functools.partial(kernel, sections, tiles),
        out_shape=(
            pltpu.VMEM((frames, prow, width, chans), BF),
            pltpu.VMEM((frames, rows, width, chans), F32),
        ),
        in_specs=[
            pl.BlockSpec(memory_space=pltpu.SMEM),
            pl.BlockSpec(memory_space=pltpu.VMEM),
            pl.BlockSpec(memory_space=pl.ANY),
            pl.BlockSpec(memory_space=pl.ANY),
            pl.BlockSpec(memory_space=pl.ANY),
            pl.BlockSpec(memory_space=pl.ANY),
        ],
        out_specs=(pl.BlockSpec(memory_space=pltpu.VMEM), pl.BlockSpec(memory_space=pltpu.VMEM)),
        scratch_shapes=[
            pltpu.VMEM((frames, rows, width, chans), BF),
            pltpu.VMEM((3, 9, chans, chans), BF),
            pltpu.VMEM((3, chans, 9 * chans), BF),
            pltpu.VMEM((9, half, chans), BF),
            pltpu.VMEM((frames, prow, width, chans), BF),
            pltpu.VMEM((16 * half, chans), BF),
            pltpu.VMEM((tall, rows, width, chans), BF),
            pltpu.VMEM((2, rows, width, chans), BF),
            pltpu.VMEM((tall, rows, width, chans), BF),
            pltpu.VMEM((frames, rows, width, chans), BF),
            pltpu.VMEM((tall * cells, 9 * chans), BF),
            pltpu.VMEM((tall * cells, 9 * chans), BF),
            pltpu.VMEM((every, 16 * half), BF),
            pltpu.VMEM((every, chans), F32),
        ] + rims(tall, rows) + rims(tall, rows) + rims(frames, rows) + rims(frames, prow) + [
            pltpu.SemaphoreType.DMA((6,)),
            pltpu.SemaphoreType.DMA((27,)),
            pltpu.SemaphoreType.DMA((2,)),
            pltpu.SemaphoreType.DMA((50,)),
            pltpu.SemaphoreType.DMA((50,)),
        ],
        compiler_params=pltpu.CompilerParams(
            collective_id=0, has_side_effects=True, vmem_limit_bytes=55 * 1024 * 1024
        ),
    )(
        frame_counts,
        norm_gain,
        latents[:, 0],
        conv_weight.reshape(27, chans, chans),
        jnp.transpose(up_weight, (0, 1, 3, 2)).reshape(9, half, chans),
        pixel_grad[:, 0],
    )
    def writer(a, b, ah, bh, sem):
        one = pltpu.make_async_copy(a, ah, sem.at[0])
        two = pltpu.make_async_copy(b, bh, sem.at[1])
        one.start()
        two.start()
        one.wait()
        two.wait()

    decoded, latent_grad = pl.pallas_call(
        writer,
        out_shape=(
            jax.ShapeDtypeStruct((frames, prow, width, chans), BF),
            jax.ShapeDtypeStruct((frames, rows, width, chans), F32),
        ),
        in_specs=[pl.BlockSpec(memory_space=pltpu.VMEM), pl.BlockSpec(memory_space=pltpu.VMEM)],
        out_specs=(pl.BlockSpec(memory_space=pl.ANY), pl.BlockSpec(memory_space=pl.ANY)),
        scratch_shapes=[pltpu.SemaphoreType.DMA((2,))],
    )(pltpu.with_memory_space_constraint(decoded, pltpu.VMEM), pltpu.with_memory_space_constraint(latent_grad, pltpu.VMEM))
    return decoded[:, None], latent_grad[:, None]


def solution(mesh):
    spec = P("section", "tile", None, None, None)
    return jax.shard_map(
        functools.partial(per_device, mesh.shape["section"], mesh.shape["tile"]),
        mesh=mesh,
        in_specs=(spec, P(), P(), P(), P(), spec),
        out_specs=(spec, spec),
        check_vma=False,
    )
```

```python
import functools

import jax
import jax.numpy as jnp
from jax import lax
from jax.experimental import pallas as pl
from jax.experimental.pallas import tpu as pltpu
from jax.sharding import PartitionSpec as P

GCOL = 4
SHIFT = GCOL + 1
EPS = 1e-06
BF = jnp.bfloat16
F32 = jnp.float32
TAPS = {-1: (2,), 0: (1, 2), 1: (0, 1), 2: (0,)}
OFFS = {0: 0, 1: 1, 2: 2, -1: 3}
UP, DOWN = (0, -1, 0), (0, 1, 0)
SIDES = tuple((0, dy, dx) for dy in (0, -1, 1) for dx in (-1, 1))
PREV, NEXT = (-1, 0, 0), (1, 0, 0)


def kernel(sections, tiles, counts, gain_ref, lat_h, cw_h, up_h, pg_h, dec, lg,
           lat, cw, up, pg, comb,
           pside, ptop, pbot, act, atop, abot, sel, seltop, selbot, araw, artop, arbot,
           graw, gh, grtop, grbot, gtop, gbot, hid, htop, hbot,
           acc, gacc, dacc, stage,
           psb, prb, prf, asb, arb, arf, alb, alf, gsb, grb, grf, hsb, hrb, hrf,
           load_sem, send_sem, recv_sem):
    frames, rows, width, chans = lat.shape
    half = up.shape[1]
    sec = lax.axis_index("section")
    tile = lax.axis_index("tile")
    place = lax.rem(tile + SHIFT, tiles)
    brow = place // GCOL
    bcol = lax.rem(place, GCOL)
    rowblocks = tiles // GCOL

    def there(ds, dy, dx):
        return (
            (sec + ds >= 0) & (sec + ds < sections)
            & (brow + dy >= 0) & (brow + dy < rowblocks)
            & (bcol + dx >= 0) & (bcol + dx < GCOL)
        )

    def who(ds, dy, dx):
        at = lax.rem(place + GCOL * dy + dx + 2 * tiles - SHIFT, tiles)
        return {"section": sec + ds, "tile": at}

    pg_in = pltpu.make_async_copy(pg_h, pg, load_sem.at[0])
    lat_in = pltpu.make_async_copy(lat_h, lat, load_sem.at[1])
    up_in = pltpu.make_async_copy(up_h, up, load_sem.at[2])
    cw_in = [pltpu.make_async_copy(cw_h.at[pl.ds(3 * k, 3)], cw.at[pl.ds(3 * k, 3)], load_sem.at[3 + k]) for k in range(9)]
    pg_in.start()
    lat_in.start()
    barrier = pltpu.get_barrier_semaphore()
    near = SIDES + (UP, DOWN, PREV, NEXT)
    for spot in near:
        @pl.when(there(*spot))
        def _(spot=spot):
            pl.semaphore_signal(barrier, inc=1, device_id=who(*spot), device_id_type=pl.DeviceIdType.MESH)

    number = [0]
    pending = []

    def message(src, dst, spot, gate=None, fill=True):
        n = number[0]
        number[0] += 1
        back = tuple(-x for x in spot)
        go, came = there(*spot), there(*back)
        if gate is not None:
            go, came = go & gate, came & gate
        copy = pltpu.make_async_remote_copy(
            src_ref=src, dst_ref=dst, send_sem=send_sem.at[n], recv_sem=recv_sem.at[n],
            device_id=who(*spot), device_id_type=pl.DeviceIdType.MESH)
        pending.append((copy, go))

        @pl.when(go)
        def _():
            copy.start()

        def arrive():
            @pl.when(came)
            def _():
                copy.wait_recv()

            if fill:
                @pl.when(jnp.logical_not(came))
                def _():
                    dst[...] = jnp.zeros(dst.shape, dst.dtype)

        return arrive

    def wait(arrivals):
        for arrive in arrivals:
            arrive()

    row_id = lax.broadcasted_iota(jnp.int32, (width, chans), 0)
    lane_id = lax.broadcasted_iota(jnp.int32, (width, chans), 1)

    def shifted(x, left, right):
        xl = jnp.where(row_id == 0, left, pltpu.roll(x, 1, axis=0))
        xr = jnp.where(row_id == width - 1, right, pltpu.roll(x, width - 1, axis=0))
        return xl, xr

    def put_edges(k, first, last):
        stage[0, pl.ds(k, 1), :] = first
        stage[1, pl.ds(k, 1), :] = last

    def pack_sides(count, sb):
        sb[...] = stage[:, pl.ds(0, count), :].astype(BF)

    def send_sides(sb, rb):
        return [
            message(sb.at[(dx + 1) // 2], rb.at[1 - dy, (1 - dx) // 2], (0, dy, dx)) for _, dy, dx in SIDES
        ]

    above, below = there(*UP), there(*DOWN)
    ways = ((0, above), (2, below))

    pg_in.wait()

    def stage_pixels(f, _):
        for r in range(rows):
            for e in range(2):
                put_edges((f * rows + r) * 2 + e, pg[f, r, e, pl.ds(0, 8)].astype(F32)[0:1],
                          pg[f, r, e, pl.ds(width - 8, 8)].astype(F32)[7:8])
        return 0

    lax.fori_loop(0, frames, stage_pixels, 0)
    pack_sides(2 * frames * rows, psb)

    length = sum(jnp.where(sec == i, counts[i], 0) for i in range(sections))
    before = sum(jnp.where(sec == i + 1, counts[i], 0) for i in range(sections - 1))
    before = jnp.maximum(before, 2)
    gain = gain_ref[...].reshape(1, chans)
    lat_in.wait()
    for load in [up_in] + cw_in:
        load.start()

    def activate(f, _):
        for r in range(rows):
            x = lat[f, r].astype(F32)
            scale = lax.rsqrt(jnp.mean(x * x, axis=-1, keepdims=True) + EPS)
            v = x * scale * gain
            a = (v * jax.nn.sigmoid(v)).astype(BF)
            act[1, f + 2, r] = a
            a = a.astype(F32)
            put_edges(f * rows + r, a[0:1], a[width - 1:width])
        return 0

    lax.fori_loop(0, frames, activate, 0)
    pack_sides(frames * rows, asb)
    for k in range(2):
        for r in range(rows):
            sel[k, r] = act[1, length + k, r]
    pl.semaphore_wait(barrier, sum(there(*spot).astype(jnp.int32) for spot in near))
    pg_sides = send_sides(psb, prb)
    act_sides = send_sides(asb, arb)
    pg_rows = [
        message(pg_h.at[:, rows - 1, 1], ptop, DOWN, fill=False),
        message(pg_h.at[:, 0, 0], pbot, UP, fill=False),
    ]
    act_ctx = [message(sel, araw, NEXT)]
    act_rows = [
        message(act.at[1, pl.ds(2, frames), rows - 1], atop.at[1, pl.ds(2, frames)], DOWN, fill=False),
        message(act.at[1, pl.ds(2, frames), 0], abot.at[1, pl.ds(2, frames)], UP, fill=False),
    ]

    up_in.wait()
    for k in range(half // 16):
        at = pl.ds(16 * k, 16)
        taps = [[up[3 * i + j, at].astype(F32) for j in range(3)] for i in range(3)]
        for v in (-1, 0, 1, 2):
            line = [functools.reduce(jnp.add, [taps[i][j] for j in TAPS[v]]) for i in range(3)]
            for u in (-1, 0, 1, 2):
                total = functools.reduce(jnp.add, [line[i] for i in TAPS[u]])
                comb[pl.ds(((u + 1) * 4 + OFFS[v]) * half + 16 * k, 16), :] = total.astype(BF)

    wait(act_sides)
    act_lat = [message(arb.at[1], alb.at[1], NEXT)]
    act_lat_rows = [message(arb.at[way], alb.at[way], NEXT, gate=has) for way, has in ways]
    wait(pg_sides)
    prf[...] = prb[...].astype(F32)

    def beside(x, left, right):
        xl, xr = shifted(x, left, right)
        return jnp.where(lane_id < half, xr, xl).astype(BF)

    def pix_spread(f, _):
        for r in range(rows):
            for e in range(2):
                k = (f * rows + r) * 2 + e
                pside[f, r, e] = beside(pg[f, r, e].astype(F32), prf[1, 0, pl.ds(k, 1), :], prf[1, 1, pl.ds(k, 1), :])
        return 0

    lax.fori_loop(0, frames, pix_spread, 0)

    def flat(x):
        return x.reshape(-1, chans)

    def cat(xs):
        return jnp.concatenate(xs, axis=1)

    def dot(a, b):
        return jnp.dot(a, b, preferred_element_type=F32)

    def dot_t(a, b):
        return lax.dot_general(a, b, (((1,), (1,)), ((), ())), preferred_element_type=F32)

    deep = 4 * half
    gacc[...] = dot(
        cat([flat(pg[:, :, 0]), flat(pside[:, :, 0]), flat(pg[:, :, 1]), flat(pside[:, :, 1])]),
        comb[pl.ds(deep, 2 * deep), :]).reshape(gacc.shape)
    inner = (frames, rows - 1, width, chans)
    gacc[:, pl.ds(1, rows - 1)] += dot(
        cat([flat(pg[:, pl.ds(0, rows - 1), 1]), flat(pside[:, pl.ds(0, rows - 1), 1])]),
        comb[pl.ds(0, deep), :]).reshape(inner)
    gacc[:, pl.ds(0, rows - 1)] += dot(
        cat([flat(pg[:, pl.ds(1, rows - 1), 0]), flat(pside[:, pl.ds(1, rows - 1), 0])]),
        comb[pl.ds(3 * deep, deep), :]).reshape(inner)

    arf[...] = arb[...].astype(F32)

    def spread_sides(buf, f, r, k, rf):
        x = buf[1, f, r].astype(F32)
        xl, xr = shifted(x, rf[1, 0, pl.ds(k, 1), :], rf[1, 1, pl.ds(k, 1), :])
        buf[0, f, r] = xl.astype(BF)
        buf[2, f, r] = xr.astype(BF)

    def act_spread(f, _):
        for r in range(rows):
            spread_sides(act, f + 2, r, f * rows + r, arf)
        return 0

    lax.fori_loop(0, frames, act_spread, 0)

    wait(pg_rows)
    line = (frames, width, chans)
    for way, has, halo, out, row, u in ((0, above, ptop, 0, 2 * rows - 1, 0), (2, below, pbot, rows - 1, 0, 3)):
        @pl.when(has)
        def _(way=way, halo=halo, out=out, row=row, u=u):
            side = [beside(halo[f].astype(F32), prf[way, 0, pl.ds(2 * rows * f + row, 1), :],
                           prf[way, 1, pl.ds(2 * rows * f + row, 1), :]) for f in range(frames)]
            gacc[:, out] += dot(cat([flat(halo[...]), jnp.concatenate(side, axis=0)]),
                                comb[pl.ds(u * deep, deep), :]).reshape(line)

    def gh_keep(f, _):
        for r in range(rows):
            x = gacc[f, r].astype(BF)
            graw[f, r] = x
            x = x.astype(F32)
            put_edges(f * rows + r, x[0:1], x[width - 1:width])
        return 0

    lax.fori_loop(0, frames, gh_keep, 0)
    pack_sides(frames * rows, gsb)
    gh_sides = send_sides(gsb, grb.at[0])
    gh_ctx = [message(graw.at[pl.ds(0, 2)], graw.at[pl.ds(frames, 2)], PREV)]
    gh_rows = [
        message(graw.at[pl.ds(0, frames), rows - 1], grtop.at[pl.ds(0, frames)], DOWN, fill=False),
        message(graw.at[pl.ds(0, frames), 0], grbot.at[pl.ds(0, frames)], UP, fill=False),
    ]

    wait(act_ctx)
    wait(act_lat)
    alf[1] = alb[1].astype(F32)
    for k in range(2):
        for r in range(rows):
            act[1, k, r] = araw[k, r]
            spread_sides(act, k, r, (before - 2 + k) * rows + r, alf)
    for load in cw_in:
        load.wait()

    def hid_main(dr):
        lo, hi = max(0, 1 - dr), min(rows, rows + 1 - dr)
        x = cat([flat(act[dc, pl.ds(dt, frames), pl.ds(lo + dr - 1, hi - lo)]) for dt in range(3) for dc in range(3)])
        w = jnp.concatenate([flat(cw[pl.ds(9 * dt + 3 * dr, 3)]) for dt in range(3)], axis=0)
        y = dot(x, w).reshape(frames, hi - lo, width, chans)
        if dr == 1:
            acc[...] = y
        else:
            acc[:, pl.ds(lo, hi - lo)] += y

    hid_main(1)
    wait(gh_sides)
    gh_lat = [message(grb.at[0, 1], grb.at[1, 1], PREV)]
    gh_lat_rows = [message(grb.at[0, way], grb.at[1, way], PREV, gate=has) for way, has in ways]

    def rim(buf, f, rf, way, k):
        x = buf[1, f].astype(F32)
        xl, xr = shifted(x, rf[way, 0, pl.ds(k, 1), :], rf[way, 1, pl.ds(k, 1), :])
        buf[0, f] = xl.astype(BF)
        buf[2, f] = xr.astype(BF)

    wait(act_rows)
    act_cor = []
    for way, has, halo, chosen, raw, row in (
            (0, above, atop, seltop, artop, rows - 1), (2, below, abot, selbot, arbot, 0)):
        @pl.when(has)
        def _(halo=halo, chosen=chosen):
            for k in range(2):
                chosen[k] = halo[1, length + k]

        act_cor.append(message(chosen, raw, NEXT, gate=has))

        @pl.when(has)
        def _(way=way, halo=halo, row=row):
            for f in range(frames):
                rim(halo, f + 2, arf, way, rows * f + row)

    hid_main(0)
    hid_main(2)
    wait(act_cor)
    wait(act_lat_rows)
    for way, has, halo, raw, out, row in ((0, above, atop, artop, 0, rows - 1), (2, below, abot, arbot, rows - 1, 0)):
        @pl.when(has)
        def _(way=way, halo=halo, raw=raw, out=out, row=row):
            alf[way] = alb[way].astype(F32)
            for k in range(2):
                halo[1, k] = raw[k]
                rim(halo, k, alf, way, (before - 2 + k) * rows + row)
            x = cat([flat(halo[dc, pl.ds(dt, frames)]) for dt in range(3) for dc in range(3)])
            w = jnp.concatenate([flat(cw[pl.ds(9 * dt + 3 * way, 3)]) for dt in range(3)], axis=0)
            acc[:, out] += dot(x, w).reshape(line)

    def hid_keep(f, _):
        for r in range(rows):
            x = acc[f, r].astype(BF)
            hid[1, f, r] = x
            x = x.astype(F32)
            put_edges(f * rows + r, x[0:1], x[width - 1:width])
        return 0

    lax.fori_loop(0, frames, hid_keep, 0)
    pack_sides(frames * rows, hsb)
    hid_sides = send_sides(hsb, hrb)
    hid_rows = [
        message(hid.at[1, :, rows - 1], htop.at[1], DOWN, fill=False),
        message(hid.at[1, :, 0], hbot.at[1], UP, fill=False),
    ]

    wait(gh_ctx)
    wait(gh_lat)
    count = frames * rows
    for g in range(2):
        for side in range(2):
            grf[1, side, pl.ds(g * count, count), :] = grb[g, 1, side].astype(F32)

    def source(f):
        return jnp.where(f < length, f, jnp.minimum(frames + f - length, frames + 1))

    def gh_spread(f, _):
        at = source(f)
        for r in range(rows):
            mid = graw[at, r]
            k = at * rows + r
            xl, xr = shifted(mid.astype(F32), grf[1, 0, pl.ds(k, 1), :], grf[1, 1, pl.ds(k, 1), :])
            gh[0, f, r] = xl.astype(BF)
            gh[1, f, r] = mid
            gh[2, f, r] = xr.astype(BF)
        return 0

    lax.fori_loop(0, frames + 2, gh_spread, 0)

    def grad_weights(dr):
        return cat([cw[9 * dt + 3 * dr + dc] for dt in range(3) for dc in range(3)])

    def grad_main(dr):
        lo, hi = max(0, dr - 1), min(rows, rows + dr - 1)
        x = cat([flat(gh[2 - dc, pl.ds(2 - dt, frames), pl.ds(lo + 1 - dr, hi - lo)])
                 for dt in range(3) for dc in range(3)])
        y = dot_t(x, grad_weights(dr)).reshape(frames, hi - lo, width, chans)
        if dr == 1:
            gacc[...] = y
        else:
            gacc[:, pl.ds(lo, hi - lo)] += y

    grad_main(1)
    wait(gh_rows)
    gh_cor = [
        message(raw.at[pl.ds(0, 2)], raw.at[pl.ds(frames, 2)], PREV, gate=has)
        for raw, has in ((grtop, above), (grbot, below))
    ]
    grad_main(0)
    grad_main(2)

    wait(hid_sides)
    hrf[...] = hrb[...].astype(F32)

    def hid_spread(f, _):
        for r in range(rows):
            spread_sides(hid, f, r, f * rows + r, hrf)
        return 0

    lax.fori_loop(0, frames, hid_spread, 0)

    def phases(a, dr, pick):
        parts = []
        u = a - 2 * (dr - 1)
        for b in range(2):
            x = cat([flat(pick(dc)) for dc in (b, b + 1)])
            w = cat([comb[pl.ds(((u + 1) * 4 + OFFS[b - 2 * (dc - 1)]) * half, half), :] for dc in (b, b + 1)])
            parts.append(dot_t(x, w))
        return cat(parts)

    for a in range(2):
        dacc[a] = phases(a, 1, lambda dc: hid[dc]).reshape(frames, rows, width, chans)
    dacc[0, :, pl.ds(1, rows - 1)] += phases(0, 0, lambda dc: hid[dc, :, pl.ds(0, rows - 1)]).reshape(inner)
    dacc[1, :, pl.ds(0, rows - 1)] += phases(1, 2, lambda dc: hid[dc, :, pl.ds(1, rows - 1)]).reshape(inner)

    def spread(f, r, a):
        real = jnp.where(f < length, 1.0, 0.0).astype(F32)
        dec[f, r, a] = (dacc[a, f, r] * real).astype(BF)

    def spread_inner(f, _):
        for r in range(rows - 1):
            spread(f, r + 1, 0)
            spread(f, r, 1)
        return 0

    lax.fori_loop(0, frames, spread_inner, 0)

    wait(gh_cor)
    wait(gh_lat_rows)
    for way, has, raw, halo, out, row in ((0, above, grtop, gtop, 0, rows - 1), (2, below, grbot, gbot, rows - 1, 0)):
        @pl.when(has)
        def _(way=way, raw=raw, halo=halo, out=out, row=row):
            for g in range(2):
                for side in range(2):
                    grf[way, side, pl.ds(g * count, count), :] = grb[g, way, side].astype(F32)
            for f in range(frames + 2):
                at = source(f)
                mid = raw[at]
                k = at * rows + row
                xl, xr = shifted(mid.astype(F32), grf[way, 0, pl.ds(k, 1), :], grf[way, 1, pl.ds(k, 1), :])
                halo[0, f] = xl.astype(BF)
                halo[1, f] = mid
                halo[2, f] = xr.astype(BF)
            x = cat([flat(halo[2 - dc, pl.ds(2 - dt, frames)]) for dt in range(3) for dc in range(3)])
            gacc[:, out] += dot_t(x, grad_weights(2 - way)).reshape(line)

    def finish(f, _):
        real = jnp.where(f < length, 1.0, 0.0).astype(F32)
        for r in range(rows):
            g = gacc[f, r]
            x = lat[f, r].astype(F32)
            scale = lax.rsqrt(jnp.mean(x * x, axis=-1, keepdims=True) + EPS)
            v = x * scale * gain
            s = jax.nn.sigmoid(v)
            dn = g * (s + v * s * (1.0 - s)) * gain
            mean = jnp.mean(dn * x, axis=-1, keepdims=True)
            lg[f, r] = (dn * scale - x * (scale * scale * scale * mean)) * real
        return 0

    lax.fori_loop(0, frames, finish, 0)

    wait(hid_rows)
    for way, has, halo, out, row, a in ((0, above, htop, 0, rows - 1, 0), (2, below, hbot, rows - 1, 0, 1)):
        @pl.when(has)
        def _(way=way, halo=halo, out=out, row=row, a=a):
            for f in range(frames):
                rim(halo, f, hrf, way, rows * f + row)
            dacc[a, :, out] += phases(a, way, lambda dc: halo[dc]).reshape(line)

    for f in range(frames):
        spread(f, 0, 0)
        spread(f, rows - 1, 1)
    for copy, went in pending:
        @pl.when(went)
        def _(copy=copy):
            copy.wait_send()


def writer(dec, lg, dec_h, lg_h, sem):
    copies = [pltpu.make_async_copy(dec, dec_h, sem.at[0]), pltpu.make_async_copy(lg, lg_h, sem.at[1])]
    for copy in copies:
        copy.start()
    for copy in copies:
        copy.wait()


def per_device(sections, tiles, latents, frame_counts, norm_gain, conv_weight, up_weight, pixel_grad):
    frames, _, rows, width, chans = latents.shape
    half = up_weight.shape[-1]
    tall = frames + 2
    count = frames * rows

    def sides(n, *context):
        return [
            pltpu.VMEM((2, n, chans), BF),
            pltpu.VMEM((*context, 3, 2, n, chans), BF),
            pltpu.VMEM((3, 2, n * (2 if context else 1), chans), F32),
        ]

    def block(*lead, dtype=BF):
        return pltpu.VMEM((*lead, width, chans), dtype)

    decoded, latent_grad = pl.pallas_call(
        functools.partial(kernel, sections, tiles),
        out_shape=(block(frames, rows, 2), block(frames, rows, dtype=F32)),
        in_specs=[
            pl.BlockSpec(memory_space=pltpu.SMEM),
            pl.BlockSpec(memory_space=pltpu.VMEM),
            pl.BlockSpec(memory_space=pl.ANY),
            pl.BlockSpec(memory_space=pl.ANY),
            pl.BlockSpec(memory_space=pl.ANY),
            pl.BlockSpec(memory_space=pl.ANY),
        ],
        out_specs=(pl.BlockSpec(memory_space=pltpu.VMEM), pl.BlockSpec(memory_space=pltpu.VMEM)),
        scratch_shapes=[
            block(frames, rows),
            pltpu.VMEM((27, chans, chans), BF),
            pltpu.VMEM((9, half, chans), BF),
            block(frames, rows, 2),
            pltpu.VMEM((16 * half, chans), BF),
            block(frames, rows, 2), block(frames), block(frames),
            block(3, tall, rows), block(3, tall), block(3, tall), block(2, rows), block(2), block(2),
            block(2, rows), block(2), block(2),
            block(tall, rows), block(3, tall, rows), block(tall), block(tall), block(3, tall), block(3, tall),
            block(3, frames, rows), block(3, frames), block(3, frames),
            block(frames, rows, dtype=F32), block(frames, rows, dtype=F32), block(2, frames, rows, dtype=F32),
            pltpu.VMEM((2, 2 * count, chans), F32),
        ] + sides(2 * count) + sides(count) + sides(count)[1:] + sides(count, 2) + sides(count) + [
            pltpu.SemaphoreType.DMA((12,)),
            pltpu.SemaphoreType.DMA((44,)),
            pltpu.SemaphoreType.DMA((44,)),
        ],
        compiler_params=pltpu.CompilerParams(
            collective_id=0, has_side_effects=True, vmem_limit_bytes=60 * 1024 * 1024
        ),
    )(
        frame_counts,
        norm_gain,
        latents[:, 0],
        conv_weight.reshape(27, chans, chans),
        jnp.transpose(up_weight, (0, 1, 3, 2)).reshape(9, half, chans),
        pixel_grad.reshape(frames, rows, 2, width, chans),
    )
    decoded, latent_grad = pl.pallas_call(
        writer,
        out_shape=(
            jax.ShapeDtypeStruct((frames, rows, 2, width, chans), BF),
            jax.ShapeDtypeStruct((frames, rows, width, chans), F32),
        ),
        in_specs=[pl.BlockSpec(memory_space=pltpu.VMEM), pl.BlockSpec(memory_space=pltpu.VMEM)],
        out_specs=(pl.BlockSpec(memory_space=pl.ANY), pl.BlockSpec(memory_space=pl.ANY)),
        scratch_shapes=[pltpu.SemaphoreType.DMA((2,))],
    )(
        pltpu.with_memory_space_constraint(decoded, pltpu.VMEM),
        pltpu.with_memory_space_constraint(latent_grad, pltpu.VMEM),
    )
    return decoded.reshape(frames, 1, 2 * rows, width, chans), latent_grad[:, None]


def solution(mesh):
    spec = P("section", "tile", None, None, None)
    return jax.shard_map(
        functools.partial(per_device, mesh.shape["section"], mesh.shape["tile"]),
        mesh=mesh,
        in_specs=(spec, P(), P(), P(), P(), spec),
        out_specs=(spec, spec),
        check_vma=False,
    )
```

```python
import functools

import jax
import jax.numpy as jnp
from jax import lax
from jax.experimental import pallas as pl
from jax.experimental.pallas import tpu as pltpu
from jax.sharding import PartitionSpec as P

GCOL = 4
SHIFT = GCOL + 1
EPS = 1e-06
BF = jnp.bfloat16
F32 = jnp.float32
TAPS = {-1: (2,), 0: (1, 2), 1: (0, 1), 2: (0,)}
OFFS = {0: 0, 1: 1, 2: 2, -1: 3}
UP, DOWN = (0, -1, 0), (0, 1, 0)
SIDES = tuple((0, dy, dx) for dy in (0, -1, 1) for dx in (-1, 1))
PREV, NEXT = (-1, 0, 0), (1, 0, 0)


def kernel(sections, tiles, counts_h, gain_h, lat_h, cw_h, up_h, pg_h, dec, lg,
           lat, cw, up, pg, comb,
           pside, ptop, pbot, act, atop, abot, sel, seltop, selbot, araw, artop, arbot,
           graw, gh, grtop, grbot, gtop, gbot, hid, htop, hbot,
           acc, gacc, dacc, stage,
           psb, prb, prf, asb, arb, arf, alb, alf, gsb, grb, grf, hsb, hrb, hrf,
           counts, gain_ref, load_sem, send_sem, recv_sem):
    frames, rows, width, chans = lat.shape
    half = up.shape[1]
    sec = lax.axis_index("section")
    tile = lax.axis_index("tile")
    place = lax.rem(tile + SHIFT, tiles)
    brow = place // GCOL
    bcol = lax.rem(place, GCOL)
    rowblocks = tiles // GCOL

    def there(ds, dy, dx):
        return (
            (sec + ds >= 0) & (sec + ds < sections)
            & (brow + dy >= 0) & (brow + dy < rowblocks)
            & (bcol + dx >= 0) & (bcol + dx < GCOL)
        )

    def who(ds, dy, dx):
        at = lax.rem(place + GCOL * dy + dx + 2 * tiles - SHIFT, tiles)
        return {"section": sec + ds, "tile": at}

    pg_in = pltpu.make_async_copy(pg_h, pg, load_sem.at[0])
    lat_in = pltpu.make_async_copy(lat_h, lat, load_sem.at[1])
    up_in = pltpu.make_async_copy(up_h, up, load_sem.at[2])
    cw_in = [pltpu.make_async_copy(cw_h.at[pl.ds(3 * k, 3)], cw.at[pl.ds(3 * k, 3)], load_sem.at[3 + k]) for k in range(9)]
    barrier = pltpu.get_barrier_semaphore()
    near = SIDES + (UP, DOWN, PREV, NEXT)
    for spot in near:
        @pl.when(there(*spot))
        def _(spot=spot):
            pl.semaphore_signal(barrier, inc=1, device_id=who(*spot), device_id_type=pl.DeviceIdType.MESH)

    small = [pltpu.make_async_copy(counts_h, counts, load_sem.at[12]), pltpu.make_async_copy(gain_h, gain_ref, load_sem.at[13])]
    for load in [pg_in, lat_in] + small + [up_in] + cw_in:
        load.start()

    number = [0]
    pending = []

    def message(src, dst, spot, gate=None, fill=True):
        n = number[0]
        number[0] += 1
        back = tuple(-x for x in spot)
        go, came = there(*spot), there(*back)
        if gate is not None:
            go, came = go & gate, came & gate
        copy = pltpu.make_async_remote_copy(
            src_ref=src, dst_ref=dst, send_sem=send_sem.at[n], recv_sem=recv_sem.at[n],
            device_id=who(*spot), device_id_type=pl.DeviceIdType.MESH)
        pending.append((copy, go))

        @pl.when(go)
        def _():
            copy.start()

        def arrive():
            @pl.when(came)
            def _():
                copy.wait_recv()

            if fill:
                @pl.when(jnp.logical_not(came))
                def _():
                    dst[...] = jnp.zeros(dst.shape, dst.dtype)

        return arrive

    def wait(arrivals):
        for arrive in arrivals:
            arrive()

    row_id = lax.broadcasted_iota(jnp.int32, (width, chans), 0)
    lane_id = lax.broadcasted_iota(jnp.int32, (width, chans), 1)

    def shifted(x, left, right):
        xl = jnp.where(row_id == 0, left, pltpu.roll(x, 1, axis=0))
        xr = jnp.where(row_id == width - 1, right, pltpu.roll(x, width - 1, axis=0))
        return xl, xr

    def put_edges(k, first, last):
        stage[0, pl.ds(k, 1), :] = first
        stage[1, pl.ds(k, 1), :] = last

    def pack_sides(count, sb):
        sb[...] = stage[:, pl.ds(0, count), :].astype(BF)

    def send_sides(sb, rb):
        return [
            message(sb.at[(dx + 1) // 2], rb.at[1 - dy, (1 - dx) // 2], (0, dy, dx)) for _, dy, dx in SIDES
        ]

    above, below = there(*UP), there(*DOWN)
    ways = ((0, above), (2, below))

    pg_in.wait()

    def stage_pixels(f, _):
        for r in range(rows):
            for e in range(2):
                put_edges((f * rows + r) * 2 + e, pg[f, r, e, pl.ds(0, 8)].astype(F32)[0:1],
                          pg[f, r, e, pl.ds(width - 8, 8)].astype(F32)[7:8])
        return 0

    lax.fori_loop(0, frames, stage_pixels, 0)
    pack_sides(2 * frames * rows, psb)

    for load in small:
        load.wait()
    length = sum(jnp.where(sec == i, counts[i], 0) for i in range(sections))
    before = sum(jnp.where(sec == i + 1, counts[i], 0) for i in range(sections - 1))
    before = jnp.maximum(before, 2)
    gain = gain_ref[...].reshape(1, chans)
    lat_in.wait()

    def activate(f, _):
        for r in range(rows):
            x = lat[f, r].astype(F32)
            scale = lax.rsqrt(jnp.mean(x * x, axis=-1, keepdims=True) + EPS)
            v = x * scale * gain
            a = (v * jax.nn.sigmoid(v)).astype(BF)
            act[1, f + 2, r] = a
            a = a.astype(F32)
            put_edges(f * rows + r, a[0:1], a[width - 1:width])
        return 0

    lax.fori_loop(0, frames, activate, 0)
    pack_sides(frames * rows, asb)
    for k in range(2):
        for r in range(rows):
            sel[k, r] = act[1, length + k, r]
    pl.semaphore_wait(barrier, sum(there(*spot).astype(jnp.int32) for spot in near))
    pg_sides = send_sides(psb, prb)
    act_sides = send_sides(asb, arb)
    pg_rows = [
        message(pg_h.at[:, rows - 1, 1], ptop, DOWN, fill=False),
        message(pg_h.at[:, 0, 0], pbot, UP, fill=False),
    ]
    act_ctx = [message(sel, araw, NEXT)]
    up_in.wait()
    for k in range(half // 16):
        at = pl.ds(16 * k, 16)
        taps = [[up[3 * i + j, at].astype(F32) for j in range(3)] for i in range(3)]
        for v in (-1, 0, 1, 2):
            line = [functools.reduce(jnp.add, [taps[i][j] for j in TAPS[v]]) for i in range(3)]
            for u in (-1, 0, 1, 2):
                total = functools.reduce(jnp.add, [line[i] for i in TAPS[u]])
                comb[pl.ds(((u + 1) * 4 + OFFS[v]) * half + 16 * k, 16), :] = total.astype(BF)

    wait(act_sides)
    act_lat = [message(arb.at[1], alb.at[1], NEXT)]
    act_lat_rows = [message(arb.at[way], alb.at[way], NEXT, gate=has) for way, has in ways]
    wait(pg_sides)
    prf[...] = prb[...].astype(F32)

    def beside(x, left, right):
        xl, xr = shifted(x, left, right)
        return jnp.where(lane_id < half, xr, xl).astype(BF)

    def pix_spread(f, _):
        for r in range(rows):
            for e in range(2):
                k = (f * rows + r) * 2 + e
                pside[f, r, e] = beside(pg[f, r, e].astype(F32), prf[1, 0, pl.ds(k, 1), :], prf[1, 1, pl.ds(k, 1), :])
        return 0

    lax.fori_loop(0, frames, pix_spread, 0)

    act_rows = [
        message(act.at[1, pl.ds(2, frames), rows - 1], atop.at[1, pl.ds(2, frames)], DOWN, fill=False),
        message(act.at[1, pl.ds(2, frames), 0], abot.at[1, pl.ds(2, frames)], UP, fill=False),
    ]

    def flat(x):
        return x.reshape(-1, chans)

    def cat(xs):
        return jnp.concatenate(xs, axis=1)

    def dot(a, b):
        return jnp.dot(a, b, preferred_element_type=F32)

    def dot_t(a, b):
        return lax.dot_general(a, b, (((1,), (1,)), ((), ())), preferred_element_type=F32)

    deep = 4 * half
    gacc[...] = dot(
        cat([flat(pg[:, :, 0]), flat(pside[:, :, 0]), flat(pg[:, :, 1]), flat(pside[:, :, 1])]),
        comb[pl.ds(deep, 2 * deep), :]).reshape(gacc.shape)
    inner = (frames, rows - 1, width, chans)
    gacc[:, pl.ds(1, rows - 1)] += dot(
        cat([flat(pg[:, pl.ds(0, rows - 1), 1]), flat(pside[:, pl.ds(0, rows - 1), 1])]),
        comb[pl.ds(0, deep), :]).reshape(inner)
    gacc[:, pl.ds(0, rows - 1)] += dot(
        cat([flat(pg[:, pl.ds(1, rows - 1), 0]), flat(pside[:, pl.ds(1, rows - 1), 0])]),
        comb[pl.ds(3 * deep, deep), :]).reshape(inner)

    arf[...] = arb[...].astype(F32)

    def spread_sides(buf, f, r, k, rf):
        x = buf[1, f, r].astype(F32)
        xl, xr = shifted(x, rf[1, 0, pl.ds(k, 1), :], rf[1, 1, pl.ds(k, 1), :])
        buf[0, f, r] = xl.astype(BF)
        buf[2, f, r] = xr.astype(BF)

    def act_spread(f, _):
        for r in range(rows):
            spread_sides(act, f + 2, r, f * rows + r, arf)
        return 0

    lax.fori_loop(0, frames, act_spread, 0)

    wait(pg_rows)
    line = (frames, width, chans)
    for way, has, halo, out, row, u in ((0, above, ptop, 0, 2 * rows - 1, 0), (2, below, pbot, rows - 1, 0, 3)):
        @pl.when(has)
        def _(way=way, halo=halo, out=out, row=row, u=u):
            side = [beside(halo[f].astype(F32), prf[way, 0, pl.ds(2 * rows * f + row, 1), :],
                           prf[way, 1, pl.ds(2 * rows * f + row, 1), :]) for f in range(frames)]
            gacc[:, out] += dot(cat([flat(halo[...]), jnp.concatenate(side, axis=0)]),
                                comb[pl.ds(u * deep, deep), :]).reshape(line)

    def gh_keep(f, _):
        for r in range(rows):
            x = gacc[f, r].astype(BF)
            graw[f, r] = x
            x = x.astype(F32)
            put_edges(f * rows + r, x[0:1], x[width - 1:width])
        return 0

    lax.fori_loop(0, frames, gh_keep, 0)
    pack_sides(frames * rows, gsb)
    gh_sides = send_sides(gsb, grb.at[0])
    gh_ctx = [message(graw.at[pl.ds(0, 2)], graw.at[pl.ds(frames, 2)], PREV)]
    gh_rows = [
        message(graw.at[pl.ds(0, frames), rows - 1], grtop.at[pl.ds(0, frames)], DOWN, fill=False),
        message(graw.at[pl.ds(0, frames), 0], grbot.at[pl.ds(0, frames)], UP, fill=False),
    ]

    wait(act_ctx)
    wait(act_lat)
    alf[1] = alb[1].astype(F32)
    for k in range(2):
        for r in range(rows):
            act[1, k, r] = araw[k, r]
            spread_sides(act, k, r, (before - 2 + k) * rows + r, alf)
    for load in cw_in:
        load.wait()

    def hid_main(dr):
        lo, hi = max(0, 1 - dr), min(rows, rows + 1 - dr)
        x = cat([flat(act[dc, pl.ds(dt, frames), pl.ds(lo + dr - 1, hi - lo)]) for dt in range(3) for dc in range(3)])
        w = jnp.concatenate([flat(cw[pl.ds(9 * dt + 3 * dr, 3)]) for dt in range(3)], axis=0)
        y = dot(x, w).reshape(frames, hi - lo, width, chans)
        if dr == 1:
            acc[...] = y
        else:
            acc[:, pl.ds(lo, hi - lo)] += y

    hid_main(1)
    wait(gh_sides)
    gh_lat = [message(grb.at[0, 1], grb.at[1, 1], PREV)]
    gh_lat_rows = [message(grb.at[0, way], grb.at[1, way], PREV, gate=has) for way, has in ways]

    def rim(buf, f, rf, way, k):
        x = buf[1, f].astype(F32)
        xl, xr = shifted(x, rf[way, 0, pl.ds(k, 1), :], rf[way, 1, pl.ds(k, 1), :])
        buf[0, f] = xl.astype(BF)
        buf[2, f] = xr.astype(BF)

    wait(act_rows)
    act_cor = []
    for way, has, halo, chosen, raw, row in (
            (0, above, atop, seltop, artop, rows - 1), (2, below, abot, selbot, arbot, 0)):
        @pl.when(has)
        def _(halo=halo, chosen=chosen):
            for k in range(2):
                chosen[k] = halo[1, length + k]

        act_cor.append(message(chosen, raw, NEXT, gate=has))

        @pl.when(has)
        def _(way=way, halo=halo, row=row):
            for f in range(frames):
                rim(halo, f + 2, arf, way, rows * f + row)

    hid_main(0)
    hid_main(2)
    wait(act_cor)
    wait(act_lat_rows)
    for way, has, halo, raw, out, row in ((0, above, atop, artop, 0, rows - 1), (2, below, abot, arbot, rows - 1, 0)):
        @pl.when(has)
        def _(way=way, halo=halo, raw=raw, out=out, row=row):
            alf[way] = alb[way].astype(F32)
            for k in range(2):
                halo[1, k] = raw[k]
                rim(halo, k, alf, way, (before - 2 + k) * rows + row)
            x = cat([flat(halo[dc, pl.ds(dt, frames)]) for dt in range(3) for dc in range(3)])
            w = jnp.concatenate([flat(cw[pl.ds(9 * dt + 3 * way, 3)]) for dt in range(3)], axis=0)
            acc[:, out] += dot(x, w).reshape(line)

    def hid_keep(f, _):
        for r in range(rows):
            x = acc[f, r].astype(BF)
            hid[1, f, r] = x
            x = x.astype(F32)
            put_edges(f * rows + r, x[0:1], x[width - 1:width])
        return 0

    lax.fori_loop(0, frames, hid_keep, 0)
    pack_sides(frames * rows, hsb)
    hid_sides = send_sides(hsb, hrb)
    hid_rows = [
        message(hid.at[1, :, rows - 1], htop.at[1], DOWN, fill=False),
        message(hid.at[1, :, 0], hbot.at[1], UP, fill=False),
    ]

    wait(gh_ctx)
    wait(gh_lat)
    count = frames * rows
    for g in range(2):
        for side in range(2):
            grf[1, side, pl.ds(g * count, count), :] = grb[g, 1, side].astype(F32)

    def source(f):
        return jnp.where(f < length, f, jnp.minimum(frames + f - length, frames + 1))

    def gh_spread(f, _):
        at = source(f)
        for r in range(rows):
            mid = graw[at, r]
            k = at * rows + r
            xl, xr = shifted(mid.astype(F32), grf[1, 0, pl.ds(k, 1), :], grf[1, 1, pl.ds(k, 1), :])
            gh[0, f, r] = xl.astype(BF)
            gh[1, f, r] = mid
            gh[2, f, r] = xr.astype(BF)
        return 0

    lax.fori_loop(0, frames + 2, gh_spread, 0)

    def grad_weights(dr):
        return cat([cw[9 * dt + 3 * dr + dc] for dt in range(3) for dc in range(3)])

    def grad_main(dr):
        lo, hi = max(0, dr - 1), min(rows, rows + dr - 1)
        x = cat([flat(gh[2 - dc, pl.ds(2 - dt, frames), pl.ds(lo + 1 - dr, hi - lo)])
                 for dt in range(3) for dc in range(3)])
        y = dot_t(x, grad_weights(dr)).reshape(frames, hi - lo, width, chans)
        if dr == 1:
            gacc[...] = y
        else:
            gacc[:, pl.ds(lo, hi - lo)] += y

    grad_main(1)
    wait(gh_rows)
    gh_cor = [
        message(raw.at[pl.ds(0, 2)], raw.at[pl.ds(frames, 2)], PREV, gate=has)
        for raw, has in ((grtop, above), (grbot, below))
    ]
    grad_main(0)
    grad_main(2)

    wait(hid_sides)
    hrf[...] = hrb[...].astype(F32)

    def hid_spread(f, _):
        for r in range(rows):
            spread_sides(hid, f, r, f * rows + r, hrf)
        return 0

    lax.fori_loop(0, frames, hid_spread, 0)

    def phases(a, dr, pick):
        parts = []
        u = a - 2 * (dr - 1)
        for b in range(2):
            x = cat([flat(pick(dc)) for dc in (b, b + 1)])
            w = cat([comb[pl.ds(((u + 1) * 4 + OFFS[b - 2 * (dc - 1)]) * half, half), :] for dc in (b, b + 1)])
            parts.append(dot_t(x, w))
        return cat(parts)

    for a in range(2):
        dacc[a] = phases(a, 1, lambda dc: hid[dc]).reshape(frames, rows, width, chans)
    dacc[0, :, pl.ds(1, rows - 1)] += phases(0, 0, lambda dc: hid[dc, :, pl.ds(0, rows - 1)]).reshape(inner)
    dacc[1, :, pl.ds(0, rows - 1)] += phases(1, 2, lambda dc: hid[dc, :, pl.ds(1, rows - 1)]).reshape(inner)

    def spread(f, r, a):
        real = jnp.where(f < length, 1.0, 0.0).astype(F32)
        dec[f, r, a] = (dacc[a, f, r] * real).astype(BF)

    def spread_inner(f, _):
        for r in range(rows - 1):
            spread(f, r + 1, 0)
            spread(f, r, 1)
        return 0

    lax.fori_loop(0, frames, spread_inner, 0)

    wait(gh_cor)
    wait(gh_lat_rows)
    for way, has, raw, halo, out, row in ((0, above, grtop, gtop, 0, rows - 1), (2, below, grbot, gbot, rows - 1, 0)):
        @pl.when(has)
        def _(way=way, raw=raw, halo=halo, out=out, row=row):
            for g in range(2):
                for side in range(2):
                    grf[way, side, pl.ds(g * count, count), :] = grb[g, way, side].astype(F32)
            for f in range(frames + 2):
                at = source(f)
                mid = raw[at]
                k = at * rows + row
                xl, xr = shifted(mid.astype(F32), grf[way, 0, pl.ds(k, 1), :], grf[way, 1, pl.ds(k, 1), :])
                halo[0, f] = xl.astype(BF)
                halo[1, f] = mid
                halo[2, f] = xr.astype(BF)
            x = cat([flat(halo[2 - dc, pl.ds(2 - dt, frames)]) for dt in range(3) for dc in range(3)])
            gacc[:, out] += dot_t(x, grad_weights(2 - way)).reshape(line)

    def finish(f, _):
        real = jnp.where(f < length, 1.0, 0.0).astype(F32)
        for r in range(rows):
            g = gacc[f, r]
            x = lat[f, r].astype(F32)
            scale = lax.rsqrt(jnp.mean(x * x, axis=-1, keepdims=True) + EPS)
            v = x * scale * gain
            s = jax.nn.sigmoid(v)
            dn = g * (s + v * s * (1.0 - s)) * gain
            mean = jnp.mean(dn * x, axis=-1, keepdims=True)
            lg[f, r] = (dn * scale - x * (scale * scale * scale * mean)) * real
        return 0

    lax.fori_loop(0, frames, finish, 0)

    wait(hid_rows)
    for way, has, halo, out, row, a in ((0, above, htop, 0, rows - 1, 0), (2, below, hbot, rows - 1, 0, 1)):
        @pl.when(has)
        def _(way=way, halo=halo, out=out, row=row, a=a):
            for f in range(frames):
                rim(halo, f, hrf, way, rows * f + row)
            dacc[a, :, out] += phases(a, way, lambda dc: halo[dc]).reshape(line)

    for f in range(frames):
        spread(f, 0, 0)
        spread(f, rows - 1, 1)
    for copy, went in pending:
        @pl.when(went)
        def _(copy=copy):
            copy.wait_send()


def writer(dec, lg, dec_h, lg_h, sem):
    copies = [pltpu.make_async_copy(dec, dec_h, sem.at[0]), pltpu.make_async_copy(lg, lg_h, sem.at[1])]
    for copy in copies:
        copy.start()
    for copy in copies:
        copy.wait()


def per_device(sections, tiles, latents, frame_counts, norm_gain, conv_weight, up_weight, pixel_grad):
    frames, _, rows, width, chans = latents.shape
    half = up_weight.shape[-1]
    tall = frames + 2
    count = frames * rows

    def sides(n, *context):
        return [
            pltpu.VMEM((2, n, chans), BF),
            pltpu.VMEM((*context, 3, 2, n, chans), BF),
            pltpu.VMEM((3, 2, n * (2 if context else 1), chans), F32),
        ]

    def block(*lead, dtype=BF):
        return pltpu.VMEM((*lead, width, chans), dtype)

    decoded, latent_grad = pl.pallas_call(
        functools.partial(kernel, sections, tiles),
        out_shape=(block(frames, rows, 2), block(frames, rows, dtype=F32)),
        in_specs=[
            pl.BlockSpec(memory_space=pl.ANY),
            pl.BlockSpec(memory_space=pl.ANY),
            pl.BlockSpec(memory_space=pl.ANY),
            pl.BlockSpec(memory_space=pl.ANY),
            pl.BlockSpec(memory_space=pl.ANY),
            pl.BlockSpec(memory_space=pl.ANY),
        ],
        out_specs=(pl.BlockSpec(memory_space=pltpu.VMEM), pl.BlockSpec(memory_space=pltpu.VMEM)),
        scratch_shapes=[
            block(frames, rows),
            pltpu.VMEM((27, chans, chans), BF),
            pltpu.VMEM((9, half, chans), BF),
            block(frames, rows, 2),
            pltpu.VMEM((16 * half, chans), BF),
            block(frames, rows, 2), block(frames), block(frames),
            block(3, tall, rows), block(3, tall), block(3, tall), block(2, rows), block(2), block(2),
            block(2, rows), block(2), block(2),
            block(tall, rows), block(3, tall, rows), block(tall), block(tall), block(3, tall), block(3, tall),
            block(3, frames, rows), block(3, frames), block(3, frames),
            block(frames, rows, dtype=F32), block(frames, rows, dtype=F32), block(2, frames, rows, dtype=F32),
            pltpu.VMEM((2, 2 * count, chans), F32),
        ] + sides(2 * count) + sides(count) + sides(count)[1:] + sides(count, 2) + sides(count) + [
            pltpu.SMEM(frame_counts.shape, jnp.int32),
            pltpu.VMEM(norm_gain.shape, F32),
            pltpu.SemaphoreType.DMA((14,)),
            pltpu.SemaphoreType.DMA((44,)),
            pltpu.SemaphoreType.DMA((44,)),
        ],
        compiler_params=pltpu.CompilerParams(
            collective_id=0, has_side_effects=True, vmem_limit_bytes=60 * 1024 * 1024
        ),
    )(
        frame_counts,
        norm_gain,
        latents[:, 0],
        conv_weight.reshape(27, chans, chans),
        jnp.transpose(up_weight, (0, 1, 3, 2)).reshape(9, half, chans),
        pixel_grad.reshape(frames, rows, 2, width, chans),
    )
    decoded, latent_grad = pl.pallas_call(
        writer,
        out_shape=(
            jax.ShapeDtypeStruct((frames, rows, 2, width, chans), BF),
            jax.ShapeDtypeStruct((frames, rows, width, chans), F32),
        ),
        in_specs=[pl.BlockSpec(memory_space=pltpu.VMEM), pl.BlockSpec(memory_space=pltpu.VMEM)],
        out_specs=(pl.BlockSpec(memory_space=pl.ANY), pl.BlockSpec(memory_space=pl.ANY)),
        scratch_shapes=[pltpu.SemaphoreType.DMA((2,))],
    )(
        pltpu.with_memory_space_constraint(decoded, pltpu.VMEM),
        pltpu.with_memory_space_constraint(latent_grad, pltpu.VMEM),
    )
    return decoded.reshape(frames, 1, 2 * rows, width, chans), latent_grad[:, None]


def solution(mesh):
    spec = P("section", "tile", None, None, None)
    return jax.shard_map(
        functools.partial(per_device, mesh.shape["section"], mesh.shape["tile"]),
        mesh=mesh,
        in_specs=(spec, P(), P(), P(), P(), spec),
        out_specs=(spec, spec),
        check_vma=False,
    )
```

```python
import functools

import jax
import jax.numpy as jnp
from jax import lax
from jax.experimental import pallas as pl
from jax.experimental.pallas import tpu as pltpu
from jax.sharding import PartitionSpec as P

GCOL = 4
SHIFT = GCOL + 1
EPS = 1e-06
BF = jnp.bfloat16
F32 = jnp.float32
TAPS = {-1: (2,), 0: (1, 2), 1: (0, 1), 2: (0,)}
OFFS = {0: 0, 1: 1, 2: 2, -1: 3}
UP, DOWN = (0, -1, 0), (0, 1, 0)
SIDES = tuple((0, dy, dx) for dy in (0, -1, 1) for dx in (-1, 1))
PREV, NEXT = (-1, 0, 0), (1, 0, 0)


def kernel(sections, tiles, counts_h, gain_h, lat_h, cw_h, up_h, pg_h, dec, lg,
           lat, cw, up, pg, comb,
           pside, ptop, pbot, act, atop, abot, sel, seltop, selbot, araw, artop, arbot,
           graw, gh, grtop, grbot, gtop, gbot, hid, htop, hbot,
           acc, gacc, dacc, stage,
           psb, prb, prf, asb, arb, arf, alb, alf, gsb, grb, grf, hsb, hrb, hrf,
           counts, gain_ref, load_sem, send_sem, recv_sem):
    frames, rows, width, chans = lat.shape
    half = up.shape[1]
    sec = lax.axis_index("section")
    tile = lax.axis_index("tile")
    place = lax.rem(tile + SHIFT, tiles)
    brow = place // GCOL
    bcol = lax.rem(place, GCOL)
    rowblocks = tiles // GCOL

    def there(ds, dy, dx):
        return (
            (sec + ds >= 0) & (sec + ds < sections)
            & (brow + dy >= 0) & (brow + dy < rowblocks)
            & (bcol + dx >= 0) & (bcol + dx < GCOL)
        )

    def who(ds, dy, dx):
        at = lax.rem(place + GCOL * dy + dx + 2 * tiles - SHIFT, tiles)
        return {"section": sec + ds, "tile": at}

    pg_in = pltpu.make_async_copy(pg_h, pg, load_sem.at[0])
    lat_in = pltpu.make_async_copy(lat_h, lat, load_sem.at[1])
    up_in = pltpu.make_async_copy(up_h, up, load_sem.at[2])
    cw_in = [pltpu.make_async_copy(cw_h.at[pl.ds(3 * k, 3)], cw.at[pl.ds(3 * k, 3)], load_sem.at[3 + k]) for k in range(9)]
    barrier = pltpu.get_barrier_semaphore()
    near = SIDES + (UP, DOWN, PREV, NEXT)
    for spot in near:
        @pl.when(there(*spot))
        def _(spot=spot):
            pl.semaphore_signal(barrier, inc=1, device_id=who(*spot), device_id_type=pl.DeviceIdType.MESH)

    small = [pltpu.make_async_copy(counts_h, counts, load_sem.at[12]), pltpu.make_async_copy(gain_h, gain_ref, load_sem.at[13])]
    for load in [pg_in, lat_in] + small + [up_in] + cw_in:
        load.start()

    number = [0]
    pending = []

    def message(src, dst, spot, gate=None, fill=True):
        n = number[0]
        number[0] += 1
        back = tuple(-x for x in spot)
        go, came = there(*spot), there(*back)
        if gate is not None:
            go, came = go & gate, came & gate
        copy = pltpu.make_async_remote_copy(
            src_ref=src, dst_ref=dst, send_sem=send_sem.at[n], recv_sem=recv_sem.at[n],
            device_id=who(*spot), device_id_type=pl.DeviceIdType.MESH)
        pending.append((copy, go))

        @pl.when(go)
        def _():
            copy.start()

        def arrive():
            @pl.when(came)
            def _():
                copy.wait_recv()

            if fill:
                @pl.when(jnp.logical_not(came))
                def _():
                    dst[...] = jnp.zeros(dst.shape, dst.dtype)

        return arrive

    def wait(arrivals):
        for arrive in arrivals:
            arrive()

    row_id = lax.broadcasted_iota(jnp.int32, (width, chans), 0)
    lane_id = lax.broadcasted_iota(jnp.int32, (width, chans), 1)

    def shifted(x, left, right):
        xl = jnp.where(row_id == 0, left, pltpu.roll(x, 1, axis=0))
        xr = jnp.where(row_id == width - 1, right, pltpu.roll(x, width - 1, axis=0))
        return xl, xr

    def put_edges(k, first, last):
        stage[0, pl.ds(k, 1), :] = first
        stage[1, pl.ds(k, 1), :] = last

    def pack_sides(count, sb):
        sb[...] = stage[:, pl.ds(0, count), :].astype(BF)

    def send_sides(sb, rb):
        return [
            message(sb.at[(dx + 1) // 2], rb.at[1 - dy, (1 - dx) // 2], (0, dy, dx)) for _, dy, dx in SIDES
        ]

    above, below = there(*UP), there(*DOWN)
    ways = ((0, above), (2, below))

    pg_in.wait()

    def stage_pixels(f, _):
        for r in range(rows):
            for e in range(2):
                put_edges((f * rows + r) * 2 + e, pg[f, r, e, pl.ds(0, 8)].astype(F32)[0:1],
                          pg[f, r, e, pl.ds(width - 8, 8)].astype(F32)[7:8])
        return 0

    lax.fori_loop(0, frames, stage_pixels, 0)
    pack_sides(2 * frames * rows, psb)

    for load in small:
        load.wait()
    length = sum(jnp.where(sec == i, counts[i], 0) for i in range(sections))
    before = sum(jnp.where(sec == i + 1, counts[i], 0) for i in range(sections - 1))
    before = jnp.maximum(before, 2)
    gain = gain_ref[...].reshape(1, chans)
    lat_in.wait()

    def activate(f, _):
        for r in range(rows):
            x = lat[f, r].astype(F32)
            scale = lax.rsqrt(jnp.mean(x * x, axis=-1, keepdims=True) + EPS)
            v = x * scale * gain
            a = (v * jax.nn.sigmoid(v)).astype(BF)
            act[1, f + 2, r] = a
            a = a.astype(F32)
            put_edges(f * rows + r, a[0:1], a[width - 1:width])
        return 0

    lax.fori_loop(0, frames, activate, 0)
    pack_sides(frames * rows, asb)
    for k in range(2):
        for r in range(rows):
            sel[k, r] = act[1, length + k, r]
    pl.semaphore_wait(barrier, sum(there(*spot).astype(jnp.int32) for spot in near))
    pg_sides = send_sides(psb, prb)
    act_sides = send_sides(asb, arb)
    pg_rows = [
        message(pg_h.at[:, rows - 1, 1], ptop, DOWN, fill=False),
        message(pg_h.at[:, 0, 0], pbot, UP, fill=False),
    ]
    act_ctx = [message(sel, araw, NEXT)]
    up_in.wait()
    for k in range(half // 16):
        at = pl.ds(16 * k, 16)
        taps = [[up[3 * i + j, at].astype(F32) for j in range(3)] for i in range(3)]
        for v in (-1, 0, 1, 2):
            line = [functools.reduce(jnp.add, [taps[i][j] for j in TAPS[v]]) for i in range(3)]
            for u in (-1, 0, 1, 2):
                total = functools.reduce(jnp.add, [line[i] for i in TAPS[u]])
                comb[pl.ds(((u + 1) * 4 + OFFS[v]) * half + 16 * k, 16), :] = total.astype(BF)

    wait(act_sides)
    act_lat = [message(arb.at[1], alb.at[1], NEXT)]
    act_lat_rows = [message(arb.at[way], alb.at[way], NEXT, gate=has) for way, has in ways]
    wait(pg_sides)
    prf[...] = prb[...].astype(F32)

    def beside(x, left, right):
        xl, xr = shifted(x, left, right)
        return jnp.where(lane_id < half, xr, xl).astype(BF)

    def pix_spread(f, _):
        for r in range(rows):
            for e in range(2):
                k = (f * rows + r) * 2 + e
                pside[f, r, e] = beside(pg[f, r, e].astype(F32), prf[1, 0, pl.ds(k, 1), :], prf[1, 1, pl.ds(k, 1), :])
        return 0

    lax.fori_loop(0, frames, pix_spread, 0)

    def flat(x):
        return x.reshape(-1, chans)

    def cat(xs):
        return jnp.concatenate(xs, axis=1)

    def dot(a, b):
        return jnp.dot(a, b, preferred_element_type=F32)

    def dot_t(a, b):
        return lax.dot_general(a, b, (((1,), (1,)), ((), ())), preferred_element_type=F32)

    deep = 4 * half
    gacc[...] = dot(
        cat([flat(pg[:, :, 0]), flat(pside[:, :, 0]), flat(pg[:, :, 1]), flat(pside[:, :, 1])]),
        comb[pl.ds(deep, 2 * deep), :]).reshape(gacc.shape)
    inner = (frames, rows - 1, width, chans)
    gacc[:, pl.ds(1, rows - 1)] += dot(
        cat([flat(pg[:, pl.ds(0, rows - 1), 1]), flat(pside[:, pl.ds(0, rows - 1), 1])]),
        comb[pl.ds(0, deep), :]).reshape(inner)
    gacc[:, pl.ds(0, rows - 1)] += dot(
        cat([flat(pg[:, pl.ds(1, rows - 1), 0]), flat(pside[:, pl.ds(1, rows - 1), 0])]),
        comb[pl.ds(3 * deep, deep), :]).reshape(inner)

    act_rows = [
        message(act.at[1, pl.ds(2, frames), rows - 1], atop.at[1, pl.ds(2, frames)], DOWN, fill=False),
        message(act.at[1, pl.ds(2, frames), 0], abot.at[1, pl.ds(2, frames)], UP, fill=False),
    ]

    arf[...] = arb[...].astype(F32)

    def spread_sides(buf, f, r, k, rf):
        x = buf[1, f, r].astype(F32)
        xl, xr = shifted(x, rf[1, 0, pl.ds(k, 1), :], rf[1, 1, pl.ds(k, 1), :])
        buf[0, f, r] = xl.astype(BF)
        buf[2, f, r] = xr.astype(BF)

    def act_spread(f, _):
        for r in range(rows):
            spread_sides(act, f + 2, r, f * rows + r, arf)
        return 0

    lax.fori_loop(0, frames, act_spread, 0)

    wait(pg_rows)
    line = (frames, width, chans)
    for way, has, halo, out, row, u in ((0, above, ptop, 0, 2 * rows - 1, 0), (2, below, pbot, rows - 1, 0, 3)):
        @pl.when(has)
        def _(way=way, halo=halo, out=out, row=row, u=u):
            side = [beside(halo[f].astype(F32), prf[way, 0, pl.ds(2 * rows * f + row, 1), :],
                           prf[way, 1, pl.ds(2 * rows * f + row, 1), :]) for f in range(frames)]
            gacc[:, out] += dot(cat([flat(halo[...]), jnp.concatenate(side, axis=0)]),
                                comb[pl.ds(u * deep, deep), :]).reshape(line)

    def gh_keep(f, _):
        for r in range(rows):
            x = gacc[f, r].astype(BF)
            graw[f, r] = x
            x = x.astype(F32)
            put_edges(f * rows + r, x[0:1], x[width - 1:width])
        return 0

    lax.fori_loop(0, frames, gh_keep, 0)
    pack_sides(frames * rows, gsb)
    gh_sides = send_sides(gsb, grb.at[0])
    gh_ctx = [message(graw.at[pl.ds(0, 2)], graw.at[pl.ds(frames, 2)], PREV)]
    gh_rows = [
        message(graw.at[pl.ds(0, frames), rows - 1], grtop.at[pl.ds(0, frames)], DOWN, fill=False),
        message(graw.at[pl.ds(0, frames), 0], grbot.at[pl.ds(0, frames)], UP, fill=False),
    ]

    wait(act_ctx)
    wait(act_lat)
    alf[1] = alb[1].astype(F32)
    for k in range(2):
        for r in range(rows):
            act[1, k, r] = araw[k, r]
            spread_sides(act, k, r, (before - 2 + k) * rows + r, alf)
    for load in cw_in:
        load.wait()

    def hid_main(dr):
        lo, hi = max(0, 1 - dr), min(rows, rows + 1 - dr)
        x = cat([flat(act[dc, pl.ds(dt, frames), pl.ds(lo + dr - 1, hi - lo)]) for dt in range(3) for dc in range(3)])
        w = jnp.concatenate([flat(cw[pl.ds(9 * dt + 3 * dr, 3)]) for dt in range(3)], axis=0)
        y = dot(x, w).reshape(frames, hi - lo, width, chans)
        if dr == 1:
            acc[...] = y
        else:
            acc[:, pl.ds(lo, hi - lo)] += y

    hid_main(1)
    wait(gh_sides)
    gh_lat = [message(grb.at[0, 1], grb.at[1, 1], PREV)]
    gh_lat_rows = [message(grb.at[0, way], grb.at[1, way], PREV, gate=has) for way, has in ways]

    def rim(buf, f, rf, way, k):
        x = buf[1, f].astype(F32)
        xl, xr = shifted(x, rf[way, 0, pl.ds(k, 1), :], rf[way, 1, pl.ds(k, 1), :])
        buf[0, f] = xl.astype(BF)
        buf[2, f] = xr.astype(BF)

    wait(act_rows)
    act_cor = []
    for way, has, halo, chosen, raw, row in (
            (0, above, atop, seltop, artop, rows - 1), (2, below, abot, selbot, arbot, 0)):
        @pl.when(has)
        def _(halo=halo, chosen=chosen):
            for k in range(2):
                chosen[k] = halo[1, length + k]

        act_cor.append(message(chosen, raw, NEXT, gate=has))

        @pl.when(has)
        def _(way=way, halo=halo, row=row):
            for f in range(frames):
                rim(halo, f + 2, arf, way, rows * f + row)

    hid_main(0)
    hid_main(2)
    wait(act_cor)
    wait(act_lat_rows)
    for way, has, halo, raw, out, row in ((0, above, atop, artop, 0, rows - 1), (2, below, abot, arbot, rows - 1, 0)):
        @pl.when(has)
        def _(way=way, halo=halo, raw=raw, out=out, row=row):
            alf[way] = alb[way].astype(F32)
            for k in range(2):
                halo[1, k] = raw[k]
                rim(halo, k, alf, way, (before - 2 + k) * rows + row)
            x = cat([flat(halo[dc, pl.ds(dt, frames)]) for dt in range(3) for dc in range(3)])
            w = jnp.concatenate([flat(cw[pl.ds(9 * dt + 3 * way, 3)]) for dt in range(3)], axis=0)
            acc[:, out] += dot(x, w).reshape(line)

    def hid_keep(f, _):
        for r in range(rows):
            x = acc[f, r].astype(BF)
            hid[1, f, r] = x
            x = x.astype(F32)
            put_edges(f * rows + r, x[0:1], x[width - 1:width])
        return 0

    lax.fori_loop(0, frames, hid_keep, 0)
    pack_sides(frames * rows, hsb)
    hid_sides = send_sides(hsb, hrb)
    hid_rows = [
        message(hid.at[1, :, rows - 1], htop.at[1], DOWN, fill=False),
        message(hid.at[1, :, 0], hbot.at[1], UP, fill=False),
    ]

    wait(gh_ctx)
    wait(gh_lat)
    count = frames * rows
    for g in range(2):
        for side in range(2):
            grf[1, side, pl.ds(g * count, count), :] = grb[g, 1, side].astype(F32)

    def source(f):
        return jnp.where(f < length, f, jnp.minimum(frames + f - length, frames + 1))

    def gh_spread(f, _):
        at = source(f)
        for r in range(rows):
            mid = graw[at, r]
            k = at * rows + r
            xl, xr = shifted(mid.astype(F32), grf[1, 0, pl.ds(k, 1), :], grf[1, 1, pl.ds(k, 1), :])
            gh[0, f, r] = xl.astype(BF)
            gh[1, f, r] = mid
            gh[2, f, r] = xr.astype(BF)
        return 0

    lax.fori_loop(0, frames + 2, gh_spread, 0)

    def grad_weights(dr):
        return cat([cw[9 * dt + 3 * dr + dc] for dt in range(3) for dc in range(3)])

    def grad_main(dr):
        lo, hi = max(0, dr - 1), min(rows, rows + dr - 1)
        x = cat([flat(gh[2 - dc, pl.ds(2 - dt, frames), pl.ds(lo + 1 - dr, hi - lo)])
                 for dt in range(3) for dc in range(3)])
        y = dot_t(x, grad_weights(dr)).reshape(frames, hi - lo, width, chans)
        if dr == 1:
            gacc[...] = y
        else:
            gacc[:, pl.ds(lo, hi - lo)] += y

    grad_main(1)
    wait(gh_rows)
    gh_cor = [
        message(raw.at[pl.ds(0, 2)], raw.at[pl.ds(frames, 2)], PREV, gate=has)
        for raw, has in ((grtop, above), (grbot, below))
    ]
    grad_main(0)
    grad_main(2)

    wait(hid_sides)
    hrf[...] = hrb[...].astype(F32)

    def hid_spread(f, _):
        for r in range(rows):
            spread_sides(hid, f, r, f * rows + r, hrf)
        return 0

    lax.fori_loop(0, frames, hid_spread, 0)

    def phases(a, dr, pick):
        parts = []
        u = a - 2 * (dr - 1)
        for b in range(2):
            x = cat([flat(pick(dc)) for dc in (b, b + 1)])
            w = cat([comb[pl.ds(((u + 1) * 4 + OFFS[b - 2 * (dc - 1)]) * half, half), :] for dc in (b, b + 1)])
            parts.append(dot_t(x, w))
        return cat(parts)

    for a in range(2):
        dacc[a] = phases(a, 1, lambda dc: hid[dc]).reshape(frames, rows, width, chans)
    dacc[0, :, pl.ds(1, rows - 1)] += phases(0, 0, lambda dc: hid[dc, :, pl.ds(0, rows - 1)]).reshape(inner)
    dacc[1, :, pl.ds(0, rows - 1)] += phases(1, 2, lambda dc: hid[dc, :, pl.ds(1, rows - 1)]).reshape(inner)

    def spread(f, r, a):
        real = jnp.where(f < length, 1.0, 0.0).astype(F32)
        dec[f, r, a] = (dacc[a, f, r] * real).astype(BF)

    def spread_inner(f, _):
        for r in range(rows - 1):
            spread(f, r + 1, 0)
            spread(f, r, 1)
        return 0

    lax.fori_loop(0, frames, spread_inner, 0)

    wait(gh_cor)
    wait(gh_lat_rows)
    for way, has, raw, halo, out, row in ((0, above, grtop, gtop, 0, rows - 1), (2, below, grbot, gbot, rows - 1, 0)):
        @pl.when(has)
        def _(way=way, raw=raw, halo=halo, out=out, row=row):
            for g in range(2):
                for side in range(2):
                    grf[way, side, pl.ds(g * count, count), :] = grb[g, way, side].astype(F32)
            for f in range(frames + 2):
                at = source(f)
                mid = raw[at]
                k = at * rows + row
                xl, xr = shifted(mid.astype(F32), grf[way, 0, pl.ds(k, 1), :], grf[way, 1, pl.ds(k, 1), :])
                halo[0, f] = xl.astype(BF)
                halo[1, f] = mid
                halo[2, f] = xr.astype(BF)
            x = cat([flat(halo[2 - dc, pl.ds(2 - dt, frames)]) for dt in range(3) for dc in range(3)])
            gacc[:, out] += dot_t(x, grad_weights(2 - way)).reshape(line)

    def finish(f, _):
        real = jnp.where(f < length, 1.0, 0.0).astype(F32)
        for r in range(rows):
            g = gacc[f, r]
            x = lat[f, r].astype(F32)
            scale = lax.rsqrt(jnp.mean(x * x, axis=-1, keepdims=True) + EPS)
            v = x * scale * gain
            s = jax.nn.sigmoid(v)
            dn = g * (s + v * s * (1.0 - s)) * gain
            mean = jnp.mean(dn * x, axis=-1, keepdims=True)
            lg[f, r] = (dn * scale - x * (scale * scale * scale * mean)) * real
        return 0

    lax.fori_loop(0, frames, finish, 0)

    wait(hid_rows)
    for way, has, halo, out, row, a in ((0, above, htop, 0, rows - 1, 0), (2, below, hbot, rows - 1, 0, 1)):
        @pl.when(has)
        def _(way=way, halo=halo, out=out, row=row, a=a):
            for f in range(frames):
                rim(halo, f, hrf, way, rows * f + row)
            dacc[a, :, out] += phases(a, way, lambda dc: halo[dc]).reshape(line)

    for f in range(frames):
        spread(f, 0, 0)
        spread(f, rows - 1, 1)
    for copy, went in pending:
        @pl.when(went)
        def _(copy=copy):
            copy.wait_send()


def writer(dec, lg, dec_h, lg_h, sem):
    copies = [pltpu.make_async_copy(dec, dec_h, sem.at[0]), pltpu.make_async_copy(lg, lg_h, sem.at[1])]
    for copy in copies:
        copy.start()
    for copy in copies:
        copy.wait()


def per_device(sections, tiles, latents, frame_counts, norm_gain, conv_weight, up_weight, pixel_grad):
    frames, _, rows, width, chans = latents.shape
    half = up_weight.shape[-1]
    tall = frames + 2
    count = frames * rows

    def sides(n, *context):
        return [
            pltpu.VMEM((2, n, chans), BF),
            pltpu.VMEM((*context, 3, 2, n, chans), BF),
            pltpu.VMEM((3, 2, n * (2 if context else 1), chans), F32),
        ]

    def block(*lead, dtype=BF):
        return pltpu.VMEM((*lead, width, chans), dtype)

    decoded, latent_grad = pl.pallas_call(
        functools.partial(kernel, sections, tiles),
        out_shape=(block(frames, rows, 2), block(frames, rows, dtype=F32)),
        in_specs=[
            pl.BlockSpec(memory_space=pl.ANY),
            pl.BlockSpec(memory_space=pl.ANY),
            pl.BlockSpec(memory_space=pl.ANY),
            pl.BlockSpec(memory_space=pl.ANY),
            pl.BlockSpec(memory_space=pl.ANY),
            pl.BlockSpec(memory_space=pl.ANY),
        ],
        out_specs=(pl.BlockSpec(memory_space=pltpu.VMEM), pl.BlockSpec(memory_space=pltpu.VMEM)),
        scratch_shapes=[
            block(frames, rows),
            pltpu.VMEM((27, chans, chans), BF),
            pltpu.VMEM((9, half, chans), BF),
            block(frames, rows, 2),
            pltpu.VMEM((16 * half, chans), BF),
            block(frames, rows, 2), block(frames), block(frames),
            block(3, tall, rows), block(3, tall), block(3, tall), block(2, rows), block(2), block(2),
            block(2, rows), block(2), block(2),
            block(tall, rows), block(3, tall, rows), block(tall), block(tall), block(3, tall), block(3, tall),
            block(3, frames, rows), block(3, frames), block(3, frames),
            block(frames, rows, dtype=F32), block(frames, rows, dtype=F32), block(2, frames, rows, dtype=F32),
            pltpu.VMEM((2, 2 * count, chans), F32),
        ] + sides(2 * count) + sides(count) + sides(count)[1:] + sides(count, 2) + sides(count) + [
            pltpu.SMEM(frame_counts.shape, jnp.int32),
            pltpu.VMEM(norm_gain.shape, F32),
            pltpu.SemaphoreType.DMA((14,)),
            pltpu.SemaphoreType.DMA((44,)),
            pltpu.SemaphoreType.DMA((44,)),
        ],
        compiler_params=pltpu.CompilerParams(
            collective_id=0, has_side_effects=True, vmem_limit_bytes=60 * 1024 * 1024
        ),
    )(
        frame_counts,
        norm_gain,
        latents[:, 0],
        conv_weight.reshape(27, chans, chans),
        jnp.transpose(up_weight, (0, 1, 3, 2)).reshape(9, half, chans),
        pixel_grad.reshape(frames, rows, 2, width, chans),
    )
    decoded, latent_grad = pl.pallas_call(
        writer,
        out_shape=(
            jax.ShapeDtypeStruct((frames, rows, 2, width, chans), BF),
            jax.ShapeDtypeStruct((frames, rows, width, chans), F32),
        ),
        in_specs=[pl.BlockSpec(memory_space=pltpu.VMEM), pl.BlockSpec(memory_space=pltpu.VMEM)],
        out_specs=(pl.BlockSpec(memory_space=pl.ANY), pl.BlockSpec(memory_space=pl.ANY)),
        scratch_shapes=[pltpu.SemaphoreType.DMA((2,))],
    )(
        pltpu.with_memory_space_constraint(decoded, pltpu.VMEM),
        pltpu.with_memory_space_constraint(latent_grad, pltpu.VMEM),
    )
    return decoded.reshape(frames, 1, 2 * rows, width, chans), latent_grad[:, None]


def solution(mesh):
    spec = P("section", "tile", None, None, None)
    return jax.shard_map(
        functools.partial(per_device, mesh.shape["section"], mesh.shape["tile"]),
        mesh=mesh,
        in_specs=(spec, P(), P(), P(), P(), spec),
        out_specs=(spec, spec),
        check_vma=False,
    )
```
